128 devices in a mesh: row: 8 (over y, x_lo), col: 16 (over z, x_hi, core).
Axes of the slice: x: 4 (x_hi: 2, x_lo: 2; x = x_hi * 2 + x_lo), y: 4, z: 4, core: 2. Of those that a mesh axis runs over, the one named last changes fastest.
Arguments:
- context_heads: bfloat16 [16384, 8192], P('row', 'col'), may hold values from -6 to 6
- teacher_proj: bfloat16 [8192, 4096], P('col', 'row'), may hold values from -0.0625 to 0.0625
- teacher_resid: bfloat16 [16384, 4096], P(('row', 'col')), may hold values from -6 to 6
- student_in: bfloat16 [16384, 1024], P(('row', 'col')), may hold values from -24 to 24
- norm_gain: bfloat16 [1024], replicated, may hold values from 0.099609375 to 1.8984375
- qkv_weight: bfloat16 [1024, 3072], replicated
- out_weight: bfloat16 [1024, 1024], replicated, may hold values from -0.1875 to 0.1875
- head_weight: bfloat16 [1024, 4096], replicated, may hold values from -0.1875 to 0.1875
- token_ids: int32 [16384], P(('row', 'col')), may hold values from 0 to 128255, as said below
- doc_ids: int32 [16384], P('row'), may hold values from 0 to 63, never falling along the last dimension, each value on 1 to 1024 neighbouring positions
Outputs:
- target: bfloat16 [16384, 4096], P(('row', 'col'))
- prediction: float32 [16384, 4096], P(('row', 'col'))
- head_grad: float32 [1024, 4096], P(('row', 'col'))
The draws below stay inside these ranges and needn't reach their ends.
Inputs may be any that keep to these rules, and one draw needn't show every extreme that they name: `token_ids`: ids of 128000 and above are special tokens that the loss skips. `doc_ids`: document numbers never fall along the whole array; a document holds at most half of 2048 positions.
All inputs are finite; a program needn't handle non-finite values.
Results may differ from the reference program's by a relative error of at most 0.012.
The reference program's roundings to bfloat16 on the way count: a program that leaves them out, or rounds other values in their place, can miss the bound.
Values may be sent and summed in bfloat16 or wider, within the bound.
No kernel may reach another device: no remote copies, remote signals or barrier semaphores. Data moves between devices by JAX's collectives and lax.ppermute only.
A program may use at most 128 MiB of HBM per device.

```python
import math
import jax
import jax.numpy as jnp
import numpy as np
from jax import lax

DIN = 8192
DOUT = 4096
DS = 1024
HEADS = 16
HEAD_DIM = 64
TOK_DEV = 128
LEN = 2048
WIN = 128
TOKENS = 16384
VOCAB = 128256
SPECIAL = 128000
N_COL = 16


def draw_token_ids(key, part):
    kind_key, drawn_key, special_key = jax.random.split(key, 3)
    kind_draw = jax.random.randint(kind_key, (TOKENS,), 0, 4)
    drawn_ids = jax.random.randint(drawn_key, (TOKENS,), 0, SPECIAL)
    special_ids = jax.random.randint(special_key, (TOKENS,), SPECIAL, VOCAB)
    token_list = jnp.where(kind_draw == 0, special_ids, drawn_ids)
    return token_list.at[0].set(VOCAB - 1).at[1].set(0)


def draw_qkv_weight(key, part):
    values = jnp.clip(jax.random.normal(key, (DS, 3 * DS), jnp.float32), -6.0, 6.0)
    return (values * DS ** (-0.5)).astype(jnp.bfloat16)


def raised(entries, rng, source, target, parts, factor):
    def block_of(axis_at):
        return (jnp.arange(entries.shape[axis_at]) // (entries.shape[axis_at] // parts)).reshape((-1,) + (1,) * (entries.ndim - 1 - axis_at))

    first = jax.random.permutation(rng, parts)[block_of(target)]
    far = (block_of(target) + parts // 2) % parts
    return jnp.where((block_of(source) == first) | (block_of(source) == far), factor * entries, entries)


def levels(rng, extent, cuts, smallest, top_value):
    factor_of = 1.0
    for axis_at, shards_of in cuts:
        steps = jax.random.uniform(jax.random.fold_in(jax.random.fold_in(rng, 6), axis_at), (shards_of,), jnp.float32, smallest / len(cuts), top_value / len(cuts))
        factor_of = factor_of * jnp.repeat(jnp.exp(steps), extent[axis_at] // shards_of).reshape((-1,) + (1,) * (len(extent) - 1 - axis_at))
    return factor_of


def length_profile(amount, total, limit, lean):
    loads = [(1 << 20) // math.isqrt(grade ** lean) + 1 for grade in range(2, amount + 1)]
    spare, holding = total - limit - (amount - 1), [1] * (amount - 1)
    while spare > 0:
        free = [i for i in range(amount - 1) if holding[i] < limit]
        whole, budget = sum([loads[i] for i in free]), spare
        for i in free:
            extra = min(limit - holding[i], max(1, budget * loads[i] // whole), spare)
            holding[i] = holding[i] + extra
            spare = spare - extra
    return np.array([limit] + holding)


def uneven_parts(key, amount, total, reach, lean):
    if amount == 2:
        one = jax.random.randint(key, (), max(1, total - reach), min(reach, total - 1) + 1)
        return jnp.stack([one, total - one])
    lengths = jnp.asarray(length_profile(amount, total, reach, lean), jnp.int32)
    twos = (amount - 1) // 2
    source_of, taker = lengths[1:1 + 2 * twos:2], lengths[2:2 + 2 * twos:2]
    room = jnp.minimum(source_of - 1, reach - taker)
    passed = jax.random.randint(jax.random.fold_in(key, 1), (twos,), 0, 1 << 20) % (room + 1)
    lengths = lengths.at[1:1 + 2 * twos:2].set(source_of - passed).at[2:2 + 2 * twos:2].set(taker + passed)
    return lengths[jax.random.permutation(jax.random.fold_in(key, 2), amount)]


def scatter_about(key, extent, spread, bound, cuts=(), kind=jnp.bfloat16):
    factor_of = levels(key, extent, cuts, -0.22, 0.18) if cuts else 1.0
    result = jax.random.normal(key, extent, jnp.float32) * spread * factor_of
    return jnp.minimum(jnp.maximum(result, -bound), bound).astype(kind)


def bell_draw_with(stream_key, dims, scale, bound, pieces, heavy, kind=jnp.bfloat16):
    values = scale * jax.random.normal(stream_key, dims, jnp.float32)
    if pieces:
        values = values * levels(stream_key, dims, pieces, -0.22, 0.18)
    return jnp.clip(raised(values, jax.random.fold_in(stream_key, 3), *heavy), -bound, bound).astype(kind)


def setup_inputs(seed: int = 0) -> dict:
    keys = jax.random.split(jax.random.key(seed), 11)
    context_heads = bell_draw_with(keys[0], (TOKENS, DIN), 1.0, 6.0, ((0, 8), (1, 16)), (1, 0, 16, 2.0))
    teacher_proj = scatter_about(keys[1], (DIN, DOUT), DIN ** -0.5, 0.0625, ((0, 16), (1, 8)))
    teacher_resid = scatter_about(keys[2], (TOKENS, DOUT), 1.0, 6.0, ((0, 128),))
    student_in = bell_draw_with(keys[3], (TOKENS, DS), 1.0, 24.0, ((0, 128),), (0, 1, 128, 5.5))
    norm_gain = jnp.clip(1.0 + 0.18 * jax.random.normal(keys[4], (DS,), jnp.float32), 0.099609375, 1.8984375).astype(jnp.bfloat16)
    qkv_weight = draw_qkv_weight(jax.random.fold_in(keys[10], 71), 0)
    out_weight = scatter_about(keys[6], (DS, DS), DS ** -0.5, 0.1875)
    head_weight = scatter_about(keys[7], (DS, DOUT), DS ** -0.5, 0.1875)
    token_ids = draw_token_ids(jax.random.fold_in(keys[10], 71), 0)
    doc_ids = jnp.searchsorted(jnp.cumsum(uneven_parts(keys[9], TOKENS // (2 * TOK_DEV), TOKENS, TOK_DEV * N_COL // 2, 1)), jnp.arange(TOKENS), side="right").astype(jnp.int32)
    return dict(context_heads=context_heads, teacher_proj=teacher_proj, teacher_resid=teacher_resid, student_in=student_in, norm_gain=norm_gain, qkv_weight=qkv_weight, out_weight=out_weight, head_weight=head_weight, token_ids=token_ids, doc_ids=doc_ids)


def reference(context_heads, teacher_proj, teacher_resid, student_in, norm_gain, qkv_weight, out_weight, head_weight, token_ids, doc_ids):
    block_width = DIN // N_COL

    def add_block(index, summed):
        first_col = index * block_width
        ctx_cols = lax.dynamic_slice_in_dim(context_heads, first_col, block_width, 1)
        weight_rows = lax.dynamic_slice_in_dim(teacher_proj, first_col, block_width, 0)
        partial_value = jnp.dot(ctx_cols, weight_rows, preferred_element_type=jnp.float32)
        return summed + lax.optimization_barrier(partial_value.astype(jnp.bfloat16)).astype(jnp.float32)
    summed = lax.fori_loop(0, N_COL, add_block, jnp.zeros((TOKENS, DOUT), jnp.float32))
    target = (teacher_resid.astype(jnp.float32) + summed).astype(jnp.bfloat16)
    student_f = student_in.astype(jnp.float32)
    mean_sq = lax.optimization_barrier(jnp.mean(student_f * student_f, axis=-1, keepdims=True))
    normed = (student_f * lax.rsqrt(mean_sq + 1e-05) * norm_gain.astype(jnp.float32)).astype(jnp.bfloat16)
    projected = jnp.dot(normed, qkv_weight, preferred_element_type=jnp.float32).astype(jnp.bfloat16)
    seq_count = TOKENS // LEN
    queries = projected[:, :DS].reshape(seq_count, LEN, HEADS, HEAD_DIM)
    keys_all = projected[:, DS:2 * DS].reshape(seq_count, LEN, HEADS, HEAD_DIM)
    values_all = projected[:, 2 * DS:].reshape(seq_count, LEN, HEADS, HEAD_DIM)
    seq_docs = doc_ids.reshape(seq_count, LEN)
    positions = jnp.arange(LEN, dtype=jnp.int32)
    in_window = jnp.abs(positions[:, None] - positions[None, :]) <= WIN

    def attend(items):
        q_seq, k_seq, v_seq, docs = items
        allowed = in_window & (docs[:, None] == docs[None, :])
        scores = jnp.einsum('qhd,khd->hqk', q_seq.astype(jnp.float32), k_seq.astype(jnp.float32)) * (1.0 / math.sqrt(HEAD_DIM))
        scores = jnp.where(allowed[None], scores, -jnp.inf)
        row_max = lax.optimization_barrier(jnp.max(scores, axis=-1, keepdims=True))
        exp_scores = jnp.exp(scores - row_max)
        weights = (exp_scores / lax.optimization_barrier(jnp.sum(exp_scores, axis=-1, keepdims=True))).astype(jnp.bfloat16)
        mixed = jnp.einsum('hqk,khd->qhd', weights.astype(jnp.float32), v_seq.astype(jnp.float32))
        return mixed.reshape(LEN, DS).astype(jnp.bfloat16)
    attended = lax.map(attend, (queries, keys_all, values_all, seq_docs)).reshape(TOKENS, DS)
    hidden = (student_f + jnp.dot(attended, out_weight, preferred_element_type=jnp.float32)).astype(jnp.bfloat16)
    prediction = jnp.dot(hidden, head_weight, preferred_element_type=jnp.float32)
    loss_mask = (token_ids < SPECIAL).astype(jnp.float32)
    scaled_error = (loss_mask[:, None] * (prediction - target.astype(jnp.float32))).astype(jnp.bfloat16)
    head_grad = jnp.dot(hidden.T, scaled_error, preferred_element_type=jnp.float32) * (1.0 / LEN)
    return (target, prediction, head_grad)
```

```python
import math

import jax
import jax.numpy as jnp
from jax import lax
from jax.experimental import pallas as pl
from jax.experimental.pallas import tpu as pltpu
from jax.sharding import Mesh
from jax.sharding import PartitionSpec as P

HEADS = 16
HEAD_DIM = 64
SPECIAL = 128000

AXES = ("y", "xl", "z", "xh", "core")
SIZES = (4, 2, 4, 2, 2)
COL = ("z", "xh", "core")


def exchange(blocks, axes):
    return lax.all_to_all(blocks, axes, 0, 0, tiled=True)


def spread(array, axes):
    size = math.prod(lax.axis_size(axis) for axis in axes)
    return exchange(jnp.broadcast_to(array[None], (size, *array.shape)), axes)


def partial_kernel(core_ref, a_ref, own_ref, other_ref, out_ref):
    core = core_ref[0]
    total = None
    for ref, side in ((own_ref, core), (other_ref, 1 - core)):
        for half in range(2):
            term = jnp.dot(
                a_ref[half, side], ref[0, 0, half], preferred_element_type=jnp.float32
            ).astype(jnp.bfloat16)
            term = term.astype(jnp.float32)
            total = term if total is None else total + term
    out_ref[0] = total.astype(jnp.bfloat16)


def teacher_partials(heads, own, other):
    _, _, tokens, depth = heads.shape
    ysize, xsize, _, _, width = own.shape
    core = lax.axis_index("core").astype(jnp.int32).reshape(1)
    weight_spec = pl.BlockSpec(
        (1, 1, 2, depth, width), lambda i, _: (i // xsize, i % xsize, 0, 0, 0)
    )
    return pl.pallas_call(
        partial_kernel,
        out_shape=jax.ShapeDtypeStruct((ysize * xsize, tokens, width), jnp.bfloat16),
        grid_spec=pltpu.PrefetchScalarGridSpec(
            num_scalar_prefetch=1,
            grid=(ysize * xsize,),
            in_specs=[
                pl.BlockSpec(heads.shape, lambda i, _: (0, 0, 0, 0)),
                weight_spec,
                weight_spec,
            ],
            out_specs=pl.BlockSpec((1, tokens, width), lambda i, _: (i, 0, 0)),
        ),
        compiler_params=pltpu.CompilerParams(vmem_limit_bytes=48 * 1024 * 1024),
        name="teacher_partials",
    )(core, heads, own, other)


def neighbours(array):
    size = math.prod(lax.axis_size(axis) for axis in COL)
    up = [(i, i + 1) for i in range(size - 1)]
    down = [(i + 1, i) for i in range(size - 1)]
    return lax.ppermute(array, COL, up), lax.ppermute(array, COL, down)


def student_hidden(student_in, norm_gain, qkv_weight, out_weight, doc_ids):
    tok_rows, student_width = student_in.shape
    student_f = student_in.astype(jnp.float32)
    mean_sq = jnp.mean(student_f * student_f, axis=-1, keepdims=True)
    normed = (student_f * lax.rsqrt(mean_sq + 1e-05) * norm_gain.astype(jnp.float32)).astype(
        jnp.bfloat16
    )
    projected = jnp.dot(normed, qkv_weight, preferred_element_type=jnp.float32).astype(jnp.bfloat16)
    queries = projected[:, :student_width].reshape(tok_rows, HEADS, HEAD_DIM)
    keyvals = projected[:, student_width:]
    before, after = neighbours(keyvals)
    widened = jnp.concatenate([before, keyvals, after], axis=0)
    keys_all = widened[:, :student_width].reshape(3 * tok_rows, HEADS, HEAD_DIM)
    values_all = widened[:, student_width:].reshape(3 * tok_rows, HEADS, HEAD_DIM)
    first_pos = lax.axis_index(COL) * tok_rows
    query_pos = first_pos + jnp.arange(tok_rows, dtype=jnp.int32)
    key_pos = first_pos - tok_rows + jnp.arange(3 * tok_rows, dtype=jnp.int32)
    filler = jnp.full((tok_rows,), -1, jnp.int32)
    padded_docs = jnp.concatenate([filler, doc_ids, filler])
    query_docs = lax.dynamic_slice_in_dim(doc_ids, first_pos, tok_rows)
    key_docs = lax.dynamic_slice_in_dim(padded_docs, first_pos, 3 * tok_rows)
    allowed = (query_docs[:, None] == key_docs[None, :]) & (
        jnp.abs(query_pos[:, None] - key_pos[None, :]) <= tok_rows
    )
    scores = jnp.einsum("qhd,khd->hqk", queries, keys_all, preferred_element_type=jnp.float32) * (
        1.0 / math.sqrt(HEAD_DIM)
    )
    scores = jnp.where(allowed[None], scores, -jnp.inf)
    row_max = jnp.max(scores, axis=-1, keepdims=True)
    exp_scores = jnp.exp(scores - row_max)
    weights = (exp_scores / jnp.sum(exp_scores, axis=-1, keepdims=True)).astype(jnp.bfloat16)
    attended = jnp.einsum("hqk,khd->qhd", weights, values_all, preferred_element_type=jnp.float32)
    attended = attended.reshape(tok_rows, student_width).astype(jnp.bfloat16)
    return (student_f + jnp.dot(attended, out_weight, preferred_element_type=jnp.float32)).astype(
        jnp.bfloat16
    )


def body(
    context_heads,
    teacher_proj,
    teacher_resid,
    student_in,
    norm_gain,
    qkv_weight,
    out_weight,
    head_weight,
    token_ids,
    doc_ids,
):
    tok_rows, student_width = student_in.shape
    row_tokens, depth = context_heads.shape
    out_width = teacher_resid.shape[1]
    width = teacher_proj.shape[1] // 2
    ysize, xlsize, zsize = (lax.axis_size(axis) for axis in ("y", "xl", "z"))
    colsize = 4 * zsize

    halves = jnp.swapaxes(teacher_proj.reshape(depth, 2, width), 0, 1)
    along_x = exchange(jnp.concatenate([halves] * xlsize), ("xl", "xh"))
    own = spread(along_x, ("y",)).reshape(ysize, xlsize, 2, depth, width)
    other = lax.ppermute(own, "core", [(0, 1), (1, 0)])

    heads = exchange(
        jnp.concatenate([context_heads.reshape(2, row_tokens // 2, depth)] * 2), ("xh", "core")
    ).reshape(2, 2, row_tokens // 2, depth)
    partials = teacher_partials(heads, own, other)
    received = exchange(partials, ("z", "core"))
    summed = jnp.sum(
        received.reshape(zsize, row_tokens, width).astype(jnp.float32), axis=0
    )

    by_owner = teacher_resid.reshape(tok_rows, zsize, 2, 2, width).transpose(1, 3, 2, 0, 4)
    resid_cols = exchange(by_owner.reshape(colsize, tok_rows, width), COL)
    target_cols = (
        resid_cols.reshape(row_tokens, width).astype(jnp.float32) + summed
    ).astype(jnp.bfloat16)
    target = exchange(target_cols.reshape(colsize, tok_rows, width), COL)
    target = target.reshape(zsize, 2, 2, tok_rows, width).transpose(3, 0, 2, 1, 4)
    target = target.reshape(tok_rows, out_width)

    hidden = student_hidden(student_in, norm_gain, qkv_weight, out_weight, doc_ids)
    prediction = jnp.dot(hidden, head_weight, preferred_element_type=jnp.float32)

    kept = jnp.where((token_ids < SPECIAL)[:, None], hidden, jnp.zeros_like(hidden))
    kept_all = spread(spread(spread(kept, ("xh",)), ("z",)), ("core",))
    kept_all = kept_all.reshape(2, zsize, 2, tok_rows, student_width).transpose(1, 2, 0, 3, 4)
    kept_all = kept_all.reshape(row_tokens, student_width)
    z, xh, core = (lax.axis_index(axis) for axis in COL)
    block = z * 4 + core * 2 + xh
    weight_cols = lax.dynamic_slice_in_dim(head_weight, block * width, width, axis=1)
    predicted = jnp.dot(kept_all, weight_cols, preferred_element_type=jnp.float32)
    error = (predicted - target_cols.astype(jnp.float32)).astype(jnp.bfloat16)
    product = lax.dot_general(
        kept_all, error, (((0,), (0,)), ((), ())), preferred_element_type=jnp.float32
    )
    everyone = math.prod(SIZES)
    pieces = exchange(product.reshape(everyone, student_width // everyone, width), AXES)
    grad = jnp.sum(
        pieces.reshape(ysize * xlsize, zsize, 2, 2, student_width // everyone, width), axis=0
    ) * (1.0 / row_tokens)
    head_grad = grad.transpose(3, 0, 2, 1, 4).reshape(student_width // everyone, out_width)
    return (target, prediction, head_grad)


def solution(mesh):
    fine = Mesh(mesh.devices.reshape(SIZES), AXES)
    row, col, whole = (("y", "xl"), COL, AXES)
    return jax.shard_map(
        body,
        mesh=fine,
        in_specs=(
            P(row, col),
            P(col, row),
            P(whole, None),
            P(whole, None),
            P(),
            P(),
            P(),
            P(),
            P(whole),
            P(row),
        ),
        out_specs=(P(whole, None), P(whole, None), P(whole, None)),
        check_vma=False,
    )
```

```python
import math

import jax
import jax.numpy as jnp
from jax import lax
from jax.experimental import pallas as pl
from jax.experimental.pallas import tpu as pltpu
from jax.sharding import Mesh
from jax.sharding import PartitionSpec as P

HEADS = 16
HEAD_DIM = 64
SPECIAL = 128000

AXES = ("y", "xl", "z", "xh", "core")
SIZES = (4, 2, 4, 2, 2)
COL = ("z", "xh", "core")
CHUNKS = 2


def exchange(blocks, axes):
    return lax.all_to_all(blocks, axes, 0, 0, tiled=True)


def shift(array, axis, step):
    size = lax.axis_size(axis)
    return lax.ppermute(array, axis, [(i, (i + step) % size) for i in range(size)])


def flip(array, *axes):
    last = 2 ** len(axes) - 1
    return lax.ppermute(array, axes, [(i, last - i) for i in range(last + 1)])


def partial_kernel(slot_ref, *refs):
    heads, weights, out_ref = refs[:4], refs[4:12], refs[12]
    width = out_ref.shape[2]
    for step in range(4):
        total = None
        for side in range(2):
            for half in range(2):
                ref = weights[side * 4 + step]
                term = jnp.dot(
                    heads[half * 2 + side][...],
                    jnp.concatenate([ref[0, half], ref[1, half]], axis=1),
                    preferred_element_type=jnp.float32,
                ).astype(jnp.bfloat16)
                term = term.astype(jnp.float32)
                total = term if total is None else total + term
        total = total.astype(jnp.bfloat16)
        for near in range(2):
            out_ref[slot_ref[step * 2 + near]] = total[:, near * width : (near + 1) * width]


def teacher_partials(slots, heads, own, other):
    tokens, depth = heads[0].shape
    width = own[0].shape[3]
    rows = 256
    weight_spec = pl.BlockSpec(own[0].shape, lambda i, _: (0, 0, 0, 0))
    return pl.pallas_call(
        partial_kernel,
        out_shape=jax.ShapeDtypeStruct((8, tokens, width), jnp.bfloat16),
        grid_spec=pltpu.PrefetchScalarGridSpec(
            num_scalar_prefetch=1,
            grid=(tokens // rows,),
            in_specs=[pl.BlockSpec((rows, depth), lambda i, _: (i, 0))] * 4 + [weight_spec] * 8,
            out_specs=pl.BlockSpec((8, rows, width), lambda i, _: (0, i, 0)),
        ),
        compiler_params=pltpu.CompilerParams(vmem_limit_bytes=48 * 1024 * 1024),
        name="teacher_partials",
    )(slots, *heads, *own, *other)


def gradient_kernel(place_ref, *refs):
    kept, parts = refs[:8], refs[8:16]
    weight_ref, resid_ref, target_ref, product_ref = refs[16:]
    rows, width = resid_ref.shape[1:]
    for far in range(4):
        for side in range(2):
            tokens = kept[far * 2 + side][...].reshape(2 * rows, -1)
            wanted = []
            for half in range(2):
                block = place_ref[(far * 2 + half) * 2 + side]
                start = pl.multiple_of((block // 2) * rows, rows)
                total = None
                for source in range(4):
                    term = parts[source * 2 + side][pl.ds(start, rows), :].astype(jnp.float32)
                    total = term if total is None else total + term
                target = (resid_ref[block].astype(jnp.float32) + total).astype(jnp.bfloat16)
                target_ref[block] = target
                wanted.append(target)
            predicted = jnp.dot(tokens, weight_ref[...], preferred_element_type=jnp.float32)
            error = (predicted - jnp.concatenate(wanted).astype(jnp.float32)).astype(jnp.bfloat16)
            term = lax.dot_general(
                tokens, error, (((0,), (0,)), ((), ())), preferred_element_type=jnp.float32
            )
            if far == 0 and side == 0:
                product_ref[...] = term
            else:
                product_ref[...] += term


def gradient_term(places, kept, parts, weight, resid):
    return pl.pallas_call(
        gradient_kernel,
        out_shape=(
            jax.ShapeDtypeStruct(resid.shape, jnp.bfloat16),
            jax.ShapeDtypeStruct(weight.shape, jnp.float32),
        ),
        grid_spec=pltpu.PrefetchScalarGridSpec(
            num_scalar_prefetch=1,
            grid=(1,),
            in_specs=[
                pl.BlockSpec(x.shape, lambda i, _, n=x.ndim: (0,) * n)
                for x in (*kept, *parts, weight, resid)
            ],
            out_specs=(
                pl.BlockSpec(resid.shape, lambda i, _: (0, 0, 0)),
                pl.BlockSpec(weight.shape, lambda i, _: (0, 0)),
            ),
        ),
        compiler_params=pltpu.CompilerParams(vmem_limit_bytes=48 * 1024 * 1024),
        name="gradient_term",
    )(places, *kept, *parts, weight, resid)


def neighbours(array):
    size = math.prod(lax.axis_size(axis) for axis in COL)
    up = [(i, (i + 1) % size) for i in range(size)]
    down = [(i, (i - 1) % size) for i in range(size)]
    return lax.ppermute(array, COL, up), lax.ppermute(array, COL, down)


def student_hidden(student_in, norm_gain, qkv_weight, out_weight, doc_ids):
    tok_rows, student_width = student_in.shape
    student_f = student_in.astype(jnp.float32)
    mean_sq = jnp.mean(student_f * student_f, axis=-1, keepdims=True)
    normed = (student_f * lax.rsqrt(mean_sq + 1e-05) * norm_gain.astype(jnp.float32)).astype(
        jnp.bfloat16
    )
    projected = jnp.dot(normed, qkv_weight, preferred_element_type=jnp.float32).astype(jnp.bfloat16)
    queries = projected[:, :student_width].reshape(tok_rows, HEADS, HEAD_DIM)
    keyvals = projected[:, student_width:]
    before, after = neighbours(keyvals)
    widened = jnp.concatenate([before, keyvals, after], axis=0)
    keys_all = widened[:, :student_width].reshape(3 * tok_rows, HEADS, HEAD_DIM)
    values_all = widened[:, student_width:].reshape(3 * tok_rows, HEADS, HEAD_DIM)
    first_pos = lax.axis_index(COL) * tok_rows
    query_pos = first_pos + jnp.arange(tok_rows, dtype=jnp.int32)
    key_pos = first_pos - tok_rows + jnp.arange(3 * tok_rows, dtype=jnp.int32)
    filler = jnp.full((tok_rows,), -1, jnp.int32)
    padded_docs = jnp.concatenate([filler, doc_ids, filler])
    query_docs = lax.dynamic_slice_in_dim(doc_ids, first_pos, tok_rows)
    key_docs = lax.dynamic_slice_in_dim(padded_docs, first_pos, 3 * tok_rows)
    allowed = (query_docs[:, None] == key_docs[None, :]) & (
        jnp.abs(query_pos[:, None] - key_pos[None, :]) <= tok_rows
    )
    scores = jnp.einsum("qhd,khd->hqk", queries, keys_all, preferred_element_type=jnp.float32) * (
        1.0 / math.sqrt(HEAD_DIM)
    )
    scores = jnp.where(allowed[None], scores, -jnp.inf)
    row_max = jnp.max(scores, axis=-1, keepdims=True)
    exp_scores = jnp.exp(scores - row_max)
    weights = (exp_scores / jnp.sum(exp_scores, axis=-1, keepdims=True)).astype(jnp.bfloat16)
    attended = jnp.einsum("hqk,khd->qhd", weights, values_all, preferred_element_type=jnp.float32)
    attended = attended.reshape(tok_rows, student_width).astype(jnp.bfloat16)
    return (student_f + jnp.dot(attended, out_weight, preferred_element_type=jnp.float32)).astype(
        jnp.bfloat16
    )


def body(
    context_heads,
    teacher_proj,
    teacher_resid,
    student_in,
    norm_gain,
    qkv_weight,
    out_weight,
    head_weight,
    token_ids,
    doc_ids,
):
    tok_rows, student_width = student_in.shape
    row_tokens, depth = context_heads.shape
    out_width = teacher_resid.shape[1]
    half_width = teacher_proj.shape[1] // 2
    width = half_width // CHUNKS
    y, xl, z, xh, core = (lax.axis_index(axis).astype(jnp.int32) for axis in AXES)

    columns = teacher_proj.reshape(depth, 2, half_width)
    mine = lax.dynamic_index_in_dim(columns, xh, 1, keepdims=False)
    theirs = lax.dynamic_index_in_dim(columns, 1 - xh, 1, keepdims=False)
    own, other = [], []
    for chunk in range(CHUNKS):
        span = slice(chunk * width, (chunk + 1) * width)
        keep, give = mine[:, span], theirs[:, span]
        across = flip(keep, "xl"), flip(give, "xh"), flip(give, "xl", "xh")
        near = jnp.stack([keep, across[1], across[0], across[2]]).reshape(2, 2, depth, width)
        along_y = [near] + [shift(near, "y", -step) for step in (1, 3, 2)]
        along_y = [along_y[i] for i in (0, 1, 3, 2)]
        own.append(along_y)
        other.append([flip(piece, "core") for piece in along_y])

    by_core = context_heads.reshape(row_tokens // (2 * tok_rows), 2, tok_rows, depth)
    here, there = (
        lax.dynamic_index_in_dim(by_core, i, 1, keepdims=False).reshape(row_tokens // 2, depth)
        for i in (core, 1 - core)
    )
    heads = (here, flip(there, "core"), flip(here, "xh"), flip(there, "xh", "core"))

    by_owner = teacher_resid.reshape(tok_rows, 4, 2, 2, half_width).transpose(1, 3, 2, 0, 4)
    resid_cols = exchange(by_owner.reshape(16, tok_rows, half_width), COL)

    hidden = student_hidden(student_in, norm_gain, qkv_weight, out_weight, doc_ids)
    prediction = jnp.dot(hidden, head_weight, preferred_element_type=jnp.float32)
    kept = jnp.where((token_ids < SPECIAL)[:, None], hidden, jnp.zeros_like(hidden))
    kept = jnp.stack([kept, flip(kept, "xh")])
    kept_all = []
    for far in range(4):
        piece = kept if far == 0 else shift(kept, "z", far)
        kept_all += [piece, flip(piece, "core")]

    steps = jnp.arange(4, dtype=jnp.int32)
    pair = jnp.arange(2, dtype=jnp.int32)
    slots = (
        ((y + steps - z) % 4)[:, None] * 2 + jnp.bitwise_xor(jnp.bitwise_xor(xl, core), pair)[None]
    ).reshape(8)
    places = (
        ((z - steps) % 4)[:, None, None] * 4
        + jnp.bitwise_xor(xh, pair)[None, :, None] * 2
        + jnp.bitwise_xor(core, pair)[None, None, :]
    ).reshape(16)
    block = z * 4 + core * 2 + xh
    targets, grads = [], []
    everyone = math.prod(SIZES)
    for chunk in range(CHUNKS):
        partials = teacher_partials(slots, heads, own[chunk], other[chunk])
        parts = []
        for far in range(4):
            for side in range(2):
                part = partials[far * 2 + side]
                if far and side:
                    moves = [
                        (i, (i // 2 + far) % 4 * 2 + 1 - i % 2) for i in range(8)
                    ]
                    part = lax.ppermute(part, ("z", "core"), moves)
                elif far:
                    part = shift(part, "z", far)
                elif side:
                    part = flip(part, "core")
                parts.append(part)
        weight = lax.dynamic_slice_in_dim(
            head_weight, block * half_width + chunk * width, width, axis=1
        )
        target_cols, product = gradient_term(
            places, kept_all, parts, weight, resid_cols[:, :, chunk * width : (chunk + 1) * width]
        )
        targets.append(exchange(target_cols, COL).reshape(4, 2, 2, tok_rows, width))
        pieces = exchange(product.reshape(everyone, student_width // everyone, width), AXES)
        grads.append(
            jnp.sum(pieces.reshape(8, 4, 2, 2, student_width // everyone, width), axis=0)
            * (1.0 / row_tokens)
        )
    target = jnp.stack(targets).transpose(4, 1, 3, 2, 0, 5).reshape(tok_rows, out_width)
    head_grad = jnp.stack(grads).transpose(4, 1, 3, 2, 0, 5).reshape(-1, out_width)
    return (target, prediction, head_grad)


def solution(mesh):
    fine = Mesh(mesh.devices.reshape(SIZES), AXES)
    row, col, whole = (("y", "xl"), COL, AXES)
    return jax.shard_map(
        body,
        mesh=fine,
        in_specs=(
            P(row, col),
            P(col, row),
            P(whole, None),
            P(whole, None),
            P(),
            P(),
            P(),
            P(),
            P(whole),
            P(row),
        ),
        out_specs=(P(whole, None), P(whole, None), P(whole, None)),
        check_vma=False,
    )
```

```python
import math

import jax
import jax.numpy as jnp
from jax import lax
from jax.experimental import pallas as pl
from jax.experimental.pallas import tpu as pltpu
from jax.sharding import Mesh
from jax.sharding import PartitionSpec as P

HEADS = 16
HEAD_DIM = 64
SPECIAL = 128000

AXES = ("y", "xl", "z", "xh", "core")
SIZES = (4, 2, 4, 2, 2)
COL = ("z", "xh", "core")
CHUNKS = 2


def exchange(blocks, axes):
    return lax.all_to_all(blocks, axes, 0, 0, tiled=True)


def shift(array, axis, step):
    size = lax.axis_size(axis)
    return lax.ppermute(array, axis, [(i, (i + step) % size) for i in range(size)])


def flip(array, *axes):
    last = 2 ** len(axes) - 1
    return lax.ppermute(array, axes, [(i, last - i) for i in range(last + 1)])


def partial_kernel(slot_ref, *refs):
    heads, weights, outs = refs[:4], refs[4:12], refs[12:20]
    sorted_ref, total_ref = refs[20:]
    width = outs[0].shape[1]

    @pl.when(pl.program_id(0) == 0)
    def _():
        for step in range(4):
            for near in range(2):
                slot = slot_ref[step * 2 + near]
                lanes = pl.ds(pl.multiple_of((slot % 2) * width, width), width)
                for side in range(2):
                    for half in range(2):
                        sorted_ref[slot // 2, side, half, :, lanes] = weights[side * 4 + step][
                            near, half
                        ]

    def step(far, carry):
        total = None
        for side in range(2):
            for half in range(2):
                term = jnp.dot(
                    heads[half * 2 + side][...],
                    sorted_ref[far, side, half],
                    preferred_element_type=jnp.float32,
                ).astype(jnp.bfloat16)
                term = term.astype(jnp.float32)
                total = term if total is None else total + term
        total_ref[far] = total.astype(jnp.bfloat16)
        return carry

    lax.fori_loop(0, 4, step, 0)
    for far in range(4):
        for side in range(2):
            outs[far * 2 + side][...] = total_ref[far, :, side * width : (side + 1) * width]


def teacher_partials(slots, heads, own, other):
    tokens, depth = heads[0].shape
    width = own[0].shape[3]
    rows = 256
    weight_spec = pl.BlockSpec(own[0].shape, lambda i, _: (0, 0, 0, 0))
    return pl.pallas_call(
        partial_kernel,
        out_shape=[jax.ShapeDtypeStruct((tokens, width), jnp.bfloat16)] * 8,
        grid_spec=pltpu.PrefetchScalarGridSpec(
            num_scalar_prefetch=1,
            grid=(tokens // rows,),
            in_specs=[pl.BlockSpec((rows, depth), lambda i, _: (i, 0))] * 4 + [weight_spec] * 8,
            out_specs=[pl.BlockSpec((rows, width), lambda i, _: (i, 0))] * 8,
            scratch_shapes=[
                pltpu.VMEM((4, 2, 2, depth, 2 * width), jnp.bfloat16),
                pltpu.VMEM((4, rows, 2 * width), jnp.bfloat16),
            ],
        ),
        compiler_params=pltpu.CompilerParams(vmem_limit_bytes=48 * 1024 * 1024),
        name="teacher_partials",
    )(slots, *heads, *own, *other)


def pack_kernel(*refs):
    pieces, outs = refs[:4], refs[4:]
    width = outs[0].shape[3]
    for chunk, out_ref in enumerate(outs):
        for i in range(4):
            out_ref[i // 2, i % 2] = pieces[i][:, chunk * width : (chunk + 1) * width]


def pack(pieces):
    depth, wide = pieces[0].shape
    shape = (2, 2, depth, wide // CHUNKS)
    return pl.pallas_call(
        pack_kernel,
        out_shape=[jax.ShapeDtypeStruct(shape, pieces[0].dtype)] * CHUNKS,
        name="pack",
    )(*pieces)


def regroup_kernel(*refs):
    for i, out_ref in enumerate(refs[4:]):
        for far in range(4):
            out_ref[far] = refs[far][i // 2, i % 2]


def regroup(pieces):
    shape = (4, *pieces[0].shape[2:])
    return pl.pallas_call(
        regroup_kernel,
        out_shape=[jax.ShapeDtypeStruct(shape, pieces[0].dtype)] * 4,
        name="regroup",
    )(*pieces)


def gradient_kernel(place_ref, *refs):
    kept, parts = refs[:8], refs[8:16]
    weight_ref, resid_ref = refs[16:18]
    targets, product_ref = refs[18:22], refs[22]
    rows = resid_ref.shape[1]
    for far in range(4):
        for side in range(2):
            tokens = kept[far * 2 + side][...].reshape(2 * rows, -1)
            wanted = []
            for half in range(2):
                block = place_ref[(far * 2 + half) * 2 + side]
                start = pl.multiple_of((block // 2) * rows, rows)
                total = None
                for source in range(4):
                    term = parts[source * 2 + side][pl.ds(start, rows), :].astype(jnp.float32)
                    total = term if total is None else total + term
                target = (resid_ref[block].astype(jnp.float32) + total).astype(jnp.bfloat16)
                targets[far][half, side] = target
                wanted.append(target)
            predicted = jnp.dot(tokens, weight_ref[...], preferred_element_type=jnp.float32)
            error = (predicted - jnp.concatenate(wanted).astype(jnp.float32)).astype(jnp.bfloat16)
            term = lax.dot_general(
                tokens, error, (((0,), (0,)), ((), ())), preferred_element_type=jnp.float32
            )
            if far == 0 and side == 0:
                product_ref[...] = term
            else:
                product_ref[...] += term


def gradient_term(places, kept, parts, weight, resid, chunk):
    rows = resid.shape[1]
    width = weight.shape[1]
    piece = (2, 2, rows, width)
    *targets, product = pl.pallas_call(
        gradient_kernel,
        out_shape=(
            *[jax.ShapeDtypeStruct(piece, jnp.bfloat16)] * 4,
            jax.ShapeDtypeStruct(weight.shape, jnp.float32),
        ),
        grid_spec=pltpu.PrefetchScalarGridSpec(
            num_scalar_prefetch=1,
            grid=(1,),
            in_specs=[
                pl.BlockSpec(x.shape, lambda i, _, n=x.ndim: (0,) * n)
                for x in (*kept, *parts, weight)
            ]
            + [pl.BlockSpec((16, rows, width), lambda i, _: (0, 0, chunk))],
            out_specs=(
                *[pl.BlockSpec(piece, lambda i, _: (0, 0, 0, 0))] * 4,
                pl.BlockSpec(weight.shape, lambda i, _: (0, 0)),
            ),
        ),
        compiler_params=pltpu.CompilerParams(vmem_limit_bytes=48 * 1024 * 1024),
        name="gradient_term",
    )(places, *kept, *parts, weight, resid)
    return targets, product


def place_kernel(column_ref, *refs):
    out_ref = refs[-1]
    for i, ref in enumerate(refs[:-1]):
        for far in range(4):
            column = pl.multiple_of(column_ref[i * 4 + far], 128)
            out_ref[:, pl.ds(column, ref.shape[2])] = ref[far]


def place_columns(columns, pieces, out_width):
    rows = pieces[0].shape[1]
    return pl.pallas_call(
        place_kernel,
        out_shape=jax.ShapeDtypeStruct((rows, out_width), pieces[0].dtype),
        grid_spec=pltpu.PrefetchScalarGridSpec(
            num_scalar_prefetch=1,
            grid=(1,),
            in_specs=[pl.BlockSpec(x.shape, lambda i, _: (0, 0, 0)) for x in pieces],
            out_specs=pl.BlockSpec((rows, out_width), lambda i, _: (0, 0)),
        ),
        name="place_columns",
    )(columns, *pieces)


def sum_kernel(scale, *refs):
    out_ref = refs[-1]
    count, _, width = refs[0].shape
    groups = 16
    for chunk, ref in enumerate(refs[:-1]):
        for place in range(groups):
            z, xh, core = place // 4, place // 2 % 2, place % 2
            total = ref[place]
            for i in range(1, count // groups):
                total = total + ref[i * groups + place]
            column = ((z * 4 + core * 2 + xh) * (len(refs) - 1) + chunk) * width
            out_ref[:, column : column + width] = total * scale


def sum_rows(pieces, out_width, scale):
    rows = pieces[0].shape[1]
    return pl.pallas_call(
        lambda *refs: sum_kernel(scale, *refs),
        out_shape=jax.ShapeDtypeStruct((rows, out_width), jnp.float32),
        name="sum_rows",
    )(*pieces)


def neighbours(array):
    size = math.prod(lax.axis_size(axis) for axis in COL)
    up = [(i, (i + 1) % size) for i in range(size)]
    down = [(i, (i - 1) % size) for i in range(size)]
    return lax.ppermute(array, COL, up), lax.ppermute(array, COL, down)


def student_hidden(student_in, norm_gain, qkv_weight, out_weight, doc_ids):
    tok_rows, student_width = student_in.shape
    student_f = student_in.astype(jnp.float32)
    mean_sq = jnp.mean(student_f * student_f, axis=-1, keepdims=True)
    normed = (student_f * lax.rsqrt(mean_sq + 1e-05) * norm_gain.astype(jnp.float32)).astype(
        jnp.bfloat16
    )
    projected = jnp.dot(normed, qkv_weight, preferred_element_type=jnp.float32).astype(jnp.bfloat16)
    queries = projected[:, :student_width].reshape(tok_rows, HEADS, HEAD_DIM)
    keyvals = projected[:, student_width:]
    before, after = neighbours(keyvals)
    widened = jnp.concatenate([before, keyvals, after], axis=0)
    keys_all = widened[:, :student_width].reshape(3 * tok_rows, HEADS, HEAD_DIM)
    values_all = widened[:, student_width:].reshape(3 * tok_rows, HEADS, HEAD_DIM)
    first_pos = lax.axis_index(COL) * tok_rows
    query_pos = first_pos + jnp.arange(tok_rows, dtype=jnp.int32)
    key_pos = first_pos - tok_rows + jnp.arange(3 * tok_rows, dtype=jnp.int32)
    filler = jnp.full((tok_rows,), -1, jnp.int32)
    padded_docs = jnp.concatenate([filler, doc_ids, filler])
    query_docs = lax.dynamic_slice_in_dim(doc_ids, first_pos, tok_rows)
    key_docs = lax.dynamic_slice_in_dim(padded_docs, first_pos, 3 * tok_rows)
    allowed = (query_docs[:, None] == key_docs[None, :]) & (
        jnp.abs(query_pos[:, None] - key_pos[None, :]) <= tok_rows
    )
    scores = jnp.einsum("qhd,khd->hqk", queries, keys_all, preferred_element_type=jnp.float32) * (
        1.0 / math.sqrt(HEAD_DIM)
    )
    scores = jnp.where(allowed[None], scores, -jnp.inf)
    row_max = jnp.max(scores, axis=-1, keepdims=True)
    exp_scores = jnp.exp(scores - row_max)
    weights = (exp_scores / jnp.sum(exp_scores, axis=-1, keepdims=True)).astype(jnp.bfloat16)
    attended = jnp.einsum("hqk,khd->qhd", weights, values_all, preferred_element_type=jnp.float32)
    attended = attended.reshape(tok_rows, student_width).astype(jnp.bfloat16)
    return (student_f + jnp.dot(attended, out_weight, preferred_element_type=jnp.float32)).astype(
        jnp.bfloat16
    )


def body(
    context_heads,
    teacher_proj,
    teacher_resid,
    student_in,
    norm_gain,
    qkv_weight,
    out_weight,
    head_weight,
    token_ids,
    doc_ids,
):
    tok_rows, student_width = student_in.shape
    row_tokens, depth = context_heads.shape
    out_width = teacher_resid.shape[1]
    half_width = teacher_proj.shape[1] // 2
    width = half_width // CHUNKS
    y, xl, z, xh, core = (lax.axis_index(axis).astype(jnp.int32) for axis in AXES)

    keep = lax.dynamic_slice_in_dim(teacher_proj, xh * half_width, half_width, axis=1)
    give = lax.dynamic_slice_in_dim(teacher_proj, (1 - xh) * half_width, half_width, axis=1)
    across = (keep, flip(give, "xh"), flip(keep, "xl"), flip(give, "xl", "xh"))
    own, other = [], []
    for near in pack(across):
        along_y = [near] + [shift(near, "y", -step) for step in (1, 3, 2)]
        along_y = [along_y[i] for i in (0, 1, 3, 2)]
        own.append(along_y)
        other.append([flip(piece, "core") for piece in along_y])

    by_core = context_heads.reshape(row_tokens // (2 * tok_rows), 2, tok_rows, depth)
    here, there = (
        lax.dynamic_index_in_dim(by_core, i, 1, keepdims=False).reshape(row_tokens // 2, depth)
        for i in (core, 1 - core)
    )
    heads = (here, flip(there, "core"), flip(here, "xh"), flip(there, "xh", "core"))

    by_owner = teacher_resid.reshape(tok_rows, 4, 2, 2, half_width).transpose(1, 3, 2, 0, 4)
    resid_cols = exchange(by_owner.reshape(16, tok_rows, half_width), COL)

    hidden = student_hidden(student_in, norm_gain, qkv_weight, out_weight, doc_ids)
    prediction = jnp.dot(hidden, head_weight, preferred_element_type=jnp.float32)
    kept = jnp.where((token_ids < SPECIAL)[:, None], hidden, jnp.zeros_like(hidden))
    kept = jnp.stack([kept, flip(kept, "xh")])
    kept_all = []
    for far in range(4):
        piece = kept if far == 0 else shift(kept, "z", far)
        kept_all += [piece, flip(piece, "core")]

    steps = jnp.arange(4, dtype=jnp.int32)
    pair = jnp.arange(2, dtype=jnp.int32)
    slots = (
        ((y + steps - z) % 4)[:, None] * 2 + jnp.bitwise_xor(jnp.bitwise_xor(xl, core), pair)[None]
    ).reshape(8)
    places = (
        ((z - steps) % 4)[:, None, None] * 4
        + jnp.bitwise_xor(xh, pair)[None, :, None] * 2
        + jnp.bitwise_xor(core, pair)[None, None, :]
    ).reshape(16)
    block = z * 4 + core * 2 + xh
    sent = [teacher_partials(slots, heads, own[i], other[i]) for i in range(CHUNKS)]
    everyone = math.prod(SIZES)
    target_pieces, columns, grad_pieces = [], [], []
    for chunk in range(CHUNKS):
        parts = []
        for far in range(4):
            for side in range(2):
                part = sent[chunk][far * 2 + side]
                if far and side:
                    moves = [(i, (i // 2 + far) % 4 * 2 + 1 - i % 2) for i in range(8)]
                    part = lax.ppermute(part, ("z", "core"), moves)
                elif far:
                    part = shift(part, "z", far)
                elif side:
                    part = flip(part, "core")
                parts.append(part)
        weight = lax.dynamic_slice_in_dim(
            head_weight, block * half_width + chunk * width, width, axis=1
        )
        targets, product = gradient_term(places, kept_all, parts, weight, resid_cols, chunk)
        grad_pieces.append(
            exchange(product.reshape(everyone, student_width // everyone, width), AXES)
        )
        targets = [targets[0]] + [shift(targets[far], "z", -far) for far in (1, 2, 3)]
        grouped = regroup(targets)
        for i, piece in enumerate(grouped):
            axes = ("xh",) * (i // 2) + ("core",) * (i % 2)
            target_pieces.append(flip(piece, *axes) if axes else piece)
            source = ((z + steps) % 4) * 4 + (core ^ (i % 2)) * 2 + (xh ^ (i // 2))
            columns.append(source * half_width + chunk * width)
    target = place_columns(jnp.concatenate(columns), target_pieces, out_width)
    head_grad = sum_rows(grad_pieces, out_width, 1.0 / row_tokens)
    return (target, prediction, head_grad)


def solution(mesh):
    fine = Mesh(mesh.devices.reshape(SIZES), AXES)
    row, col, whole = (("y", "xl"), COL, AXES)
    return jax.shard_map(
        body,
        mesh=fine,
        in_specs=(
            P(row, col),
            P(col, row),
            P(whole, None),
            P(whole, None),
            P(),
            P(),
            P(),
            P(),
            P(whole),
            P(row),
        ),
        out_specs=(P(whole, None), P(whole, None), P(whole, None)),
        check_vma=False,
    )
```

```python
import math

import jax
import jax.numpy as jnp
from jax import lax
from jax.experimental import pallas as pl
from jax.experimental.pallas import tpu as pltpu
from jax.sharding import Mesh
from jax.sharding import PartitionSpec as P

HEADS = 16
HEAD_DIM = 64
SPECIAL = 128000

AXES = ("y", "xl", "zh", "zl", "xh", "core")
SIZES = (4, 2, 2, 2, 2, 2)
COL = ("zh", "zl", "xh", "core")
Z = ("zh", "zl")
CHUNKS = 2


def exchange(blocks, axes):
    return lax.all_to_all(blocks, axes, 0, 0, tiled=True)


def shift(array, axes, step):
    size = math.prod(lax.axis_size(axis) for axis in axes)
    return lax.ppermute(array, axes, [(i, (i + step) % size) for i in range(size)])


def flip(array, *axes):
    last = 2 ** len(axes) - 1
    return lax.ppermute(array, axes, [(i, last - i) for i in range(last + 1)])


def partial_kernel(slot_ref, *refs):
    heads, weights, outs = refs[:4], refs[4:-10], refs[-10:-2]
    sorted_ref, total_ref = refs[-2:]
    if len(weights) == 6:
        weights = (*weights[:5], *[weights[5].at[i] for i in range(3)])
    width = outs[0].shape[1]

    @pl.when(pl.program_id(0) == 0)
    def _():
        for step in range(4):
            for near in range(2):
                slot = slot_ref[step * 2 + near]
                lanes = pl.ds(pl.multiple_of((slot % 2) * width, width), width)
                for side in range(2):
                    for half in range(2):
                        sorted_ref[slot // 2, side, half, :, lanes] = weights[side * 4 + step][
                            near, half
                        ]

    def step(far, carry):
        total = None
        for side in range(2):
            for half in range(2):
                term = jnp.dot(
                    heads[half * 2 + side][...],
                    sorted_ref[far, side, half],
                    preferred_element_type=jnp.float32,
                ).astype(jnp.bfloat16)
                term = term.astype(jnp.float32)
                total = term if total is None else total + term
        total_ref[far] = total.astype(jnp.bfloat16)
        return carry

    lax.fori_loop(0, 4, step, 0)
    for far in range(4):
        for side in range(2):
            outs[far * 2 + side][...] = total_ref[far, :, side * width : (side + 1) * width]


def teacher_partials(slots, heads, own, other, chunk):
    tokens, depth = heads[0].shape
    width = own[0].shape[3]
    rows = 512
    weight_spec = pl.BlockSpec(own[0].shape, lambda i, _: (0, 0, 0, 0))
    return pl.pallas_call(
        partial_kernel,
        out_shape=[jax.ShapeDtypeStruct((tokens, width), jnp.bfloat16)] * 8,
        grid_spec=pltpu.PrefetchScalarGridSpec(
            num_scalar_prefetch=1,
            grid=(tokens // rows,),
            in_specs=[pl.BlockSpec((rows, depth), lambda i, _: (i, 0))] * 4
            + [weight_spec] * 4
            + [pl.BlockSpec((None, *own[0].shape), lambda i, _: (chunk, 0, 0, 0, 0))]
            + [
                pl.BlockSpec(x.shape, lambda i, _, n=x.ndim: (0,) * n)
                for x in other[1:]
            ],
            out_specs=[pl.BlockSpec((rows, width), lambda i, _: (i, 0))] * 8,
            scratch_shapes=[
                pltpu.VMEM((4, 2, 2, depth, 2 * width), jnp.bfloat16),
                pltpu.VMEM((4, rows, 2 * width), jnp.bfloat16),
            ],
        ),
        compiler_params=pltpu.CompilerParams(vmem_limit_bytes=58 * 1024 * 1024),
        name="teacher_partials",
    )(slots, *heads, *own, *other)


def pack_kernel(*refs):
    pieces, whole_ref, outs = refs[:4], refs[4], refs[5:]
    width = outs[0].shape[3]
    for chunk, out_ref in enumerate(outs):
        for i in range(4):
            piece = pieces[i][:, chunk * width : (chunk + 1) * width]
            out_ref[i // 2, i % 2] = piece
            whole_ref[chunk, i // 2, i % 2] = piece


def pack(pieces):
    depth, wide = pieces[0].shape
    shape = (2, 2, depth, wide // CHUNKS)
    return pl.pallas_call(
        pack_kernel,
        out_shape=[
            jax.ShapeDtypeStruct((CHUNKS, *shape), pieces[0].dtype),
            *[jax.ShapeDtypeStruct(shape, pieces[0].dtype)] * CHUNKS,
        ],
        name="pack",
    )(*pieces)


def regroup_kernel(*refs):
    for i, out_ref in enumerate(refs[4:]):
        for far in range(4):
            out_ref[far] = refs[far][i // 2, i % 2]


def regroup(pieces):
    shape = (4, *pieces[0].shape[2:])
    return pl.pallas_call(
        regroup_kernel,
        out_shape=[jax.ShapeDtypeStruct(shape, pieces[0].dtype)] * 4,
        name="regroup",
    )(*pieces)


def gradient_kernel(place_ref, *refs):
    kept, parts = refs[:2], refs[2 : 2 + 8 * CHUNKS]
    weight_ref, resid_ref = refs[-8:-6]
    targets, product_ref, target_ref = refs[-6:-2], refs[-2], refs[-1]
    rows = resid_ref.shape[1]
    product_ref[...] = jnp.zeros_like(product_ref)

    def step(far, carry):
        for side in range(2):
            tokens = kept[side][far].reshape(2 * rows, -1)
            wanted = []
            for half in range(2):
                block = place_ref[(far * 2 + half) * 2 + side]
                start = pl.multiple_of((block // 2) * rows, rows)
                sums = []
                for chunk in range(CHUNKS):
                    total = None
                    for source in range(4):
                        part = parts[chunk * 8 + source * 2 + side]
                        term = part[pl.ds(start, rows), :].astype(jnp.float32)
                        total = term if total is None else total + term
                    sums.append(total)
                total = jnp.concatenate(sums, axis=1)
                target = (resid_ref[block].astype(jnp.float32) + total).astype(jnp.bfloat16)
                target_ref[far, half, side] = target
                wanted.append(target)
            predicted = jnp.dot(tokens, weight_ref[...], preferred_element_type=jnp.float32)
            error = (predicted - jnp.concatenate(wanted).astype(jnp.float32)).astype(jnp.bfloat16)
            product_ref[...] += lax.dot_general(
                tokens, error, (((0,), (0,)), ((), ())), preferred_element_type=jnp.float32
            )
        return carry

    lax.fori_loop(0, 4, step, 0)
    for far in range(4):
        targets[far][...] = target_ref[far]


def gradient_term(places, kept, parts, weight, resid):
    rows = resid.shape[1]
    width = weight.shape[1]
    piece = (2, 2, rows, width)
    *targets, product = pl.pallas_call(
        gradient_kernel,
        out_shape=(
            *[jax.ShapeDtypeStruct(piece, jnp.bfloat16)] * 4,
            jax.ShapeDtypeStruct(weight.shape, jnp.float32),
        ),
        grid_spec=pltpu.PrefetchScalarGridSpec(
            num_scalar_prefetch=1,
            grid=(1,),
            in_specs=[
                pl.BlockSpec(x.shape, lambda i, _, n=x.ndim: (0,) * n)
                for x in (*kept, *parts, weight, resid)
            ],
            out_specs=(
                *[pl.BlockSpec(piece, lambda i, _: (0, 0, 0, 0))] * 4,
                pl.BlockSpec(weight.shape, lambda i, _: (0, 0)),
            ),
            scratch_shapes=[pltpu.VMEM((4, *piece), jnp.bfloat16)],
        ),
        compiler_params=pltpu.CompilerParams(vmem_limit_bytes=58 * 1024 * 1024),
        name="gradient_term",
    )(places, *kept, *parts, weight, resid)
    return targets, product


def place_kernel(column_ref, *refs):
    out_ref = refs[-1]
    for i, ref in enumerate(refs[:-1]):
        for far in range(4):
            column = pl.multiple_of(column_ref[i * 4 + far], 128)
            out_ref[:, pl.ds(column, ref.shape[2])] = ref[far]


def place_columns(columns, pieces, out_width):
    rows = pieces[0].shape[1]
    return pl.pallas_call(
        place_kernel,
        out_shape=jax.ShapeDtypeStruct((rows, out_width), pieces[0].dtype),
        grid_spec=pltpu.PrefetchScalarGridSpec(
            num_scalar_prefetch=1,
            grid=(1,),
            in_specs=[pl.BlockSpec(x.shape, lambda i, _: (0, 0, 0)) for x in pieces],
            out_specs=pl.BlockSpec((rows, out_width), lambda i, _: (0, 0)),
        ),
        name="place_columns",
    )(columns, *pieces)


def sum_kernel(scale, *refs):
    out_ref = refs[-1]
    count, _, width = refs[0].shape
    groups = 16
    for chunk, ref in enumerate(refs[:-1]):
        for place in range(groups):
            zh, zl, owner = place // 8, place // 4 % 2, place % 4
            total = ref[place]
            for i in range(1, count // groups):
                total = total + ref[i * groups + place]
            column = ((zh * 8 + owner * 2 + zl) * (len(refs) - 1) + chunk) * width
            out_ref[:, column : column + width] = total * scale


def sum_rows(pieces, out_width, scale):
    rows = pieces[0].shape[1]
    return pl.pallas_call(
        lambda *refs: sum_kernel(scale, *refs),
        out_shape=jax.ShapeDtypeStruct((rows, out_width), jnp.float32),
        name="sum_rows",
    )(*pieces)


def neighbours(array):
    return shift(array, COL, 1), shift(array, COL, -1)


def normed_rows(rows, norm_gain):
    rows_f = rows.astype(jnp.float32)
    mean_sq = jnp.mean(rows_f * rows_f, axis=-1, keepdims=True)
    return (rows_f * lax.rsqrt(mean_sq + 1e-05) * norm_gain.astype(jnp.float32)).astype(
        jnp.bfloat16
    )


def student_hidden(widened_in, norm_gain, qkv_weight, out_weight, doc_ids):
    tok_rows, student_width = widened_in.shape[0] // 3, widened_in.shape[1]
    student_f = widened_in[tok_rows : 2 * tok_rows].astype(jnp.float32)
    normed = normed_rows(widened_in, norm_gain)
    widened = jnp.dot(
        normed, qkv_weight[:, student_width:], preferred_element_type=jnp.float32
    ).astype(jnp.bfloat16)
    queries = jnp.dot(
        normed[tok_rows : 2 * tok_rows],
        qkv_weight[:, :student_width],
        preferred_element_type=jnp.float32,
    ).astype(jnp.bfloat16)
    queries = queries.reshape(tok_rows, HEADS, HEAD_DIM)
    keys_all = widened[:, :student_width].reshape(3 * tok_rows, HEADS, HEAD_DIM)
    values_all = widened[:, student_width:].reshape(3 * tok_rows, HEADS, HEAD_DIM)
    first_pos = lax.axis_index(COL) * tok_rows
    query_pos = first_pos + jnp.arange(tok_rows, dtype=jnp.int32)
    key_pos = first_pos - tok_rows + jnp.arange(3 * tok_rows, dtype=jnp.int32)
    filler = jnp.full((tok_rows,), -1, jnp.int32)
    padded_docs = jnp.concatenate([filler, doc_ids, filler])
    query_docs = lax.dynamic_slice_in_dim(doc_ids, first_pos, tok_rows)
    key_docs = lax.dynamic_slice_in_dim(padded_docs, first_pos, 3 * tok_rows)
    allowed = (query_docs[:, None] == key_docs[None, :]) & (
        jnp.abs(query_pos[:, None] - key_pos[None, :]) <= tok_rows
    )
    scores = jnp.einsum("qhd,khd->hqk", queries, keys_all, preferred_element_type=jnp.float32) * (
        1.0 / math.sqrt(HEAD_DIM)
    )
    scores = jnp.where(allowed[None], scores, -jnp.inf)
    row_max = jnp.max(scores, axis=-1, keepdims=True)
    exp_scores = jnp.exp(scores - row_max)
    weights = (exp_scores / jnp.sum(exp_scores, axis=-1, keepdims=True)).astype(jnp.bfloat16)
    attended = jnp.einsum("hqk,khd->qhd", weights, values_all, preferred_element_type=jnp.float32)
    attended = attended.reshape(tok_rows, student_width).astype(jnp.bfloat16)
    return (student_f + jnp.dot(attended, out_weight, preferred_element_type=jnp.float32)).astype(
        jnp.bfloat16
    )


def body(
    context_heads,
    teacher_proj,
    teacher_resid,
    student_in,
    norm_gain,
    qkv_weight,
    out_weight,
    head_weight,
    token_ids,
    doc_ids,
):
    tok_rows, student_width = student_in.shape
    row_tokens, depth = context_heads.shape
    out_width = teacher_resid.shape[1]
    half_width = teacher_proj.shape[1] // 2
    y, xl, zh, zl, xh, core = (lax.axis_index(axis).astype(jnp.int32) for axis in AXES)
    z, owner = zh * 2 + zl, zh * 2 + xh

    keep = lax.dynamic_slice_in_dim(teacher_proj, zl * half_width, half_width, axis=1)
    give = lax.dynamic_slice_in_dim(teacher_proj, (1 - zl) * half_width, half_width, axis=1)
    across = (keep, flip(give, "zl"), flip(keep, "xl"), flip(give, "xl", "zl"))
    own, other = [], []
    whole, *nears = pack(across)
    whole = flip(whole, "core")
    for chunk, near in enumerate(nears):
        along_y = [near] + [shift(near, ("y",), -step) for step in (1, 3, 2)]
        along_y = [along_y[i] for i in (0, 1, 3, 2)]
        own.append(along_y)
        if chunk:
            stack = jnp.stack(along_y[1:])
            other.append((whole, flip(stack, "core")))
        else:
            other.append([whole] + [flip(piece, "core") for piece in along_y[1:]])

    by_core = context_heads.reshape(row_tokens // (2 * tok_rows), 2, tok_rows, depth)
    here, there = (
        lax.dynamic_index_in_dim(by_core, i, 1, keepdims=False).reshape(row_tokens // 2, depth)
        for i in (core, 1 - core)
    )
    heads = (here, flip(there, "core"), flip(here, "zl"), flip(there, "zl", "core"))

    by_owner = teacher_resid.reshape(tok_rows, 2, 2, 2, 2, half_width).transpose(1, 4, 2, 3, 0, 5)
    resid_cols = exchange(by_owner.reshape(16, tok_rows, half_width), COL)

    before, after = neighbours(student_in)
    widened_in = jnp.concatenate([before, student_in, after])
    hidden = student_hidden(widened_in, norm_gain, qkv_weight, out_weight, doc_ids)
    prediction = jnp.dot(hidden, head_weight, preferred_element_type=jnp.float32)
    kept = jnp.where((token_ids < SPECIAL)[:, None], hidden, jnp.zeros_like(hidden))
    kept = jnp.stack([kept, flip(kept, "xh")])
    from_z = [shift(kept, Z, far) for far in (1, 2, 3)]
    kept = jnp.stack([kept, *from_z])
    kept_all = (kept, flip(kept, "core"))

    steps = jnp.arange(4, dtype=jnp.int32)
    pair = jnp.arange(2, dtype=jnp.int32)
    slots = (
        jnp.bitwise_xor((y + steps) % 4, owner)[:, None] * 2
        + jnp.bitwise_xor(jnp.bitwise_xor(xl, core), pair)[None]
    ).reshape(8)
    places = (
        ((z - steps) % 4)[:, None, None] * 4
        + jnp.bitwise_xor(xh, pair)[None, :, None] * 2
        + jnp.bitwise_xor(core, pair)[None, None, :]
    ).reshape(16)
    block = (owner * 2 + core) * 2 + zl
    sent = []
    for chunk in range(CHUNKS):
        sent.append(teacher_partials(slots, heads, own[chunk], other[chunk], chunk))
    everyone = math.prod(SIZES)
    parts = []
    for chunk in range(CHUNKS):
        for far in range(4):
            for side in range(2):
                axes = ("zh",) * (far // 2) + ("xh",) * (far % 2) + ("core",) * side
                part = sent[chunk][far * 2 + side]
                parts.append(flip(part, *axes) if axes else part)
    weight = lax.dynamic_slice_in_dim(head_weight, block * half_width, half_width, axis=1)
    targets, product = gradient_term(places, kept_all, parts, weight, resid_cols)
    grad_pieces = exchange(product.reshape(everyone, student_width // everyone, half_width), AXES)
    head_grad = sum_rows([grad_pieces], out_width, 1.0 / row_tokens)
    targets = [targets[0]] + [shift(targets[far], Z, -far) for far in (1, 2, 3)]
    grouped = regroup(targets)
    target_pieces, columns = [], []
    for i, piece in enumerate(grouped):
        axes = ("xh",) * (i // 2) + ("core",) * (i % 2)
        target_pieces.append(flip(piece, *axes) if axes else piece)
        from_z = (z + steps) % 4
        source = from_z // 2 * 8 + (xh ^ (i // 2)) * 4 + (core ^ (i % 2)) * 2 + from_z % 2
        columns.append(source * half_width)
    target = place_columns(jnp.concatenate(columns), target_pieces, out_width)
    return (target, prediction, head_grad)


def solution(mesh):
    fine = Mesh(mesh.devices.reshape(SIZES), AXES)
    row, col, whole = (("y", "xl"), COL, AXES)
    return jax.shard_map(
        body,
        mesh=fine,
        in_specs=(
            P(row, col),
            P(col, row),
            P(whole, None),
            P(whole, None),
            P(),
            P(),
            P(),
            P(),
            P(whole),
            P(row),
        ),
        out_specs=(P(whole, None), P(whole, None), P(whole, None)),
        check_vma=False,
    )
```

```python
import math

import jax
import jax.numpy as jnp
from jax import lax
from jax.experimental import pallas as pl
from jax.experimental.pallas import tpu as pltpu
from jax.sharding import Mesh
from jax.sharding import PartitionSpec as P

HEAD_DIM = 64
SPECIAL = 128000

AXES = ("y", "xl", "zh", "zl", "xh", "core")
SIZES = (4, 2, 2, 2, 2, 2)
COL = ("zh", "zl", "xh", "core")
Z = ("zh", "zl")
CHUNKS = 2


def exchange(blocks, axes):
    return lax.all_to_all(blocks, axes, 0, 0, tiled=True)


def shift(array, axes, step):
    size = math.prod(lax.axis_size(axis) for axis in axes)
    return lax.ppermute(array, axes, [(i, (i + step) % size) for i in range(size)])


def flip(array, *axes):
    last = 2 ** len(axes) - 1
    return lax.ppermute(array, axes, [(i, last - i) for i in range(last + 1)])


def partial_kernel(slot_ref, *refs):
    heads, weights, outs = refs[:4], refs[4:12], refs[12:16]
    sorted_ref, total_ref = refs[16:]
    width = outs[0].shape[1] // 2

    @pl.when(pl.program_id(0) == 0)
    def _():
        for step in range(4):
            for near in range(2):
                slot = slot_ref[step * 2 + near]
                lanes = pl.ds(pl.multiple_of((slot % 2) * width, width), width)
                for side in range(2):
                    for half in range(2):
                        sorted_ref[slot // 2, side, half, :, lanes] = weights[side * 4 + step][
                            near, half
                        ]

    def step(far, carry):
        total = None
        for side in range(2):
            for half in range(2):
                term = jnp.dot(
                    heads[half * 2 + side][...],
                    sorted_ref[far, side, half],
                    preferred_element_type=jnp.float32,
                ).astype(jnp.bfloat16)
                term = term.astype(jnp.float32)
                total = term if total is None else total + term
        total_ref[far] = total.astype(jnp.bfloat16)
        return carry

    lax.fori_loop(0, 4, step, 0)
    for far in range(4):
        outs[far][...] = total_ref[far]


def teacher_partials(slots, heads, own, other, chunk):
    tokens, depth = heads[0].shape
    width = own[0].shape[3]
    rows = 512
    weight_spec = pl.BlockSpec(own[0].shape, lambda i, _: (0, 0, 0, 0))
    return pl.pallas_call(
        partial_kernel,
        out_shape=[jax.ShapeDtypeStruct((tokens, 2 * width), jnp.bfloat16)] * 4,
        grid_spec=pltpu.PrefetchScalarGridSpec(
            num_scalar_prefetch=1,
            grid=(tokens // rows,),
            in_specs=[pl.BlockSpec((rows, depth), lambda i, _: (i, 0))] * 4
            + [weight_spec] * 4
            + [pl.BlockSpec((None, *own[0].shape), lambda i, _: (chunk, 0, 0, 0, 0))]
            + [
                pl.BlockSpec(x.shape, lambda i, _, n=x.ndim: (0,) * n)
                for x in other[1:]
            ],
            out_specs=[pl.BlockSpec((rows, 2 * width), lambda i, _: (i, 0))] * 4,
            scratch_shapes=[
                pltpu.VMEM((4, 2, 2, depth, 2 * width), jnp.bfloat16),
                pltpu.VMEM((4, rows, 2 * width), jnp.bfloat16),
            ],
        ),
        compiler_params=pltpu.CompilerParams(vmem_limit_bytes=58 * 1024 * 1024),
        name="teacher_partials",
    )(slots, *heads, *own, *other)


def pack_kernel(*refs):
    pieces, whole_ref, outs = refs[:4], refs[4], refs[5:]
    width = outs[0].shape[3]
    for chunk, out_ref in enumerate(outs):
        for i in range(4):
            piece = pieces[i][:, chunk * width : (chunk + 1) * width]
            out_ref[i // 2, i % 2] = piece
            whole_ref[chunk, i // 2, i % 2] = piece


def pack(pieces):
    depth, wide = pieces[0].shape
    shape = (2, 2, depth, wide // CHUNKS)
    return pl.pallas_call(
        pack_kernel,
        out_shape=[
            jax.ShapeDtypeStruct((CHUNKS, *shape), pieces[0].dtype),
            *[jax.ShapeDtypeStruct(shape, pieces[0].dtype)] * CHUNKS,
        ],
        name="pack",
    )(*pieces)


def regroup_kernel(*refs):
    for half, out_ref in enumerate(refs[4:]):
        for far in range(4):
            out_ref[far] = refs[far][half]


def regroup(pieces):
    shape = (4, *pieces[0].shape[1:])
    return pl.pallas_call(
        regroup_kernel,
        out_shape=[jax.ShapeDtypeStruct(shape, pieces[0].dtype)] * 2,
        name="regroup",
    )(*pieces)


def gradient_kernel(place_ref, kept_ref, *refs):
    parts = refs[: 4 * CHUNKS]
    weight_ref, resid_ref = refs[4 * CHUNKS : 4 * CHUNKS + 2]
    targets, (own_ref, give_ref), (target_ref, product_ref) = refs[-8:-4], refs[-4:-2], refs[-2:]
    rows, wide = resid_ref.shape[1:]
    width = wide // 2
    piece = width // CHUNKS
    core = place_ref[8]
    product_ref[...] = jnp.zeros_like(product_ref)

    def step(far, carry):
        tokens = kept_ref[far].reshape(2 * rows, -1)
        wanted = []
        for half in range(2):
            block = place_ref[far * 2 + half]
            start = pl.multiple_of(block * rows, rows)
            sums = []
            for side in range(2):
                for chunk in range(CHUNKS):
                    total = None
                    for source in range(4):
                        part = parts[chunk * 4 + source]
                        lanes = slice(side * piece, (side + 1) * piece)
                        term = part[pl.ds(start, rows), lanes].astype(jnp.float32)
                        total = term if total is None else total + term
                    sums.append(total)
            resid = [
                resid_ref[block, :, pl.ds(pl.multiple_of(column * width, width), width)]
                for column in (core, 1 - core)
            ]
            resid = jnp.concatenate(resid, axis=1).astype(jnp.float32)
            target = (resid + jnp.concatenate(sums, axis=1)).astype(jnp.bfloat16)
            target_ref[far, half] = target
            wanted.append(target)
        predicted = jnp.dot(tokens, weight_ref[...], preferred_element_type=jnp.float32)
        error = (predicted - jnp.concatenate(wanted).astype(jnp.float32)).astype(jnp.bfloat16)
        product_ref[...] += lax.dot_general(
            tokens, error, (((0,), (0,)), ((), ())), preferred_element_type=jnp.float32
        )
        return carry

    lax.fori_loop(0, 4, step, 0)
    for far in range(4):
        targets[far][...] = target_ref[far]
    own_ref[...] = product_ref[:, :width]
    give_ref[...] = product_ref[:, width:]


def gradient_term(places, kept, parts, weight, resid):
    rows, wide = resid.shape[1:]
    piece = (2, rows, wide)
    half = (weight.shape[0], wide // 2)
    *targets, own, give = pl.pallas_call(
        gradient_kernel,
        out_shape=(
            *[jax.ShapeDtypeStruct(piece, jnp.bfloat16)] * 4,
            *[jax.ShapeDtypeStruct(half, jnp.float32)] * 2,
        ),
        grid_spec=pltpu.PrefetchScalarGridSpec(
            num_scalar_prefetch=1,
            grid=(1,),
            in_specs=[
                pl.BlockSpec(x.shape, lambda i, _, n=x.ndim: (0,) * n)
                for x in (kept, *parts, weight, resid)
            ],
            out_specs=(
                *[pl.BlockSpec(piece, lambda i, _: (0, 0, 0))] * 4,
                *[pl.BlockSpec(half, lambda i, _: (0, 0))] * 2,
            ),
            scratch_shapes=[
                pltpu.VMEM((4, *piece), jnp.bfloat16),
                pltpu.VMEM(weight.shape, jnp.float32),
            ],
        ),
        compiler_params=pltpu.CompilerParams(vmem_limit_bytes=58 * 1024 * 1024),
        name="gradient_term",
    )(places, kept, *parts, weight, resid)
    return targets, own, give


def place_kernel(column_ref, *refs):
    out_ref = refs[-1]
    width = refs[0].shape[2] // 2
    for i, ref in enumerate(refs[:-1]):
        for far in range(4):
            for side in range(2):
                column = pl.multiple_of(column_ref[(i * 4 + far) * 2 + side], width)
                out_ref[:, pl.ds(column, width)] = ref[far, :, side * width : (side + 1) * width]


def place_columns(columns, pieces, out_width):
    rows = pieces[0].shape[1]
    return pl.pallas_call(
        place_kernel,
        out_shape=jax.ShapeDtypeStruct((rows, out_width), pieces[0].dtype),
        grid_spec=pltpu.PrefetchScalarGridSpec(
            num_scalar_prefetch=1,
            grid=(1,),
            in_specs=[pl.BlockSpec(x.shape, lambda i, _: (0, 0, 0)) for x in pieces],
            out_specs=pl.BlockSpec((rows, out_width), lambda i, _: (0, 0)),
        ),
        name="place_columns",
    )(columns, *pieces)


def sum_kernel(scale, *refs):
    out_ref = refs[-1]
    count, _, width = refs[0].shape
    groups = 16
    for chunk, ref in enumerate(refs[:-1]):
        for place in range(groups):
            zh, zl, owner = place // 8, place // 4 % 2, place % 4
            total = ref[place]
            for i in range(1, count // groups):
                total = total + ref[i * groups + place]
            column = ((zh * 8 + owner * 2 + zl) * (len(refs) - 1) + chunk) * width
            out_ref[:, column : column + width] = total * scale


def sum_rows(pieces, out_width, scale):
    rows = pieces[0].shape[1]
    return pl.pallas_call(
        lambda *refs: sum_kernel(scale, *refs),
        out_shape=jax.ShapeDtypeStruct((rows, out_width), jnp.float32),
        name="sum_rows",
    )(*pieces)


def neighbours(array):
    return shift(array, COL, 1), shift(array, COL, -1)


def normed_rows(rows, norm_gain):
    rows_f = rows.astype(jnp.float32)
    mean_sq = jnp.mean(rows_f * rows_f, axis=-1, keepdims=True)
    return (rows_f * lax.rsqrt(mean_sq + 1e-05) * norm_gain.astype(jnp.float32)).astype(
        jnp.bfloat16
    )


def attend_kernel(query_ref, keyval_ref, allowed_ref, out_ref):
    tok_rows, width = query_ref.shape
    pair = 2 * HEAD_DIM
    allowed = allowed_ref[...] > 0.0
    lane = lax.broadcasted_iota(jnp.int32, (tok_rows, pair), 1)
    for first in range(0, width, pair):
        queries = query_ref[:, first : first + pair]
        keys = keyval_ref[:, first : first + pair]
        values = keyval_ref[:, width + first : width + first + pair]
        mixed = []
        for head in range(2):
            inside = (lane < HEAD_DIM) if head == 0 else (lane >= HEAD_DIM)
            mine = jnp.where(inside, queries.astype(jnp.float32), 0.0).astype(jnp.bfloat16)
            scores = lax.dot_general(
                mine, keys, (((1,), (1,)), ((), ())), preferred_element_type=jnp.float32
            ) * (1.0 / math.sqrt(HEAD_DIM))
            scores = jnp.where(allowed, scores, -jnp.inf)
            exp_scores = jnp.exp(scores - jnp.max(scores, axis=-1, keepdims=True))
            weights = exp_scores / jnp.sum(exp_scores, axis=-1, keepdims=True)
            mixed.append(
                jnp.dot(
                    weights.astype(jnp.bfloat16), values, preferred_element_type=jnp.float32
                )
            )
        out = jnp.where(lane < HEAD_DIM, mixed[0], mixed[1])
        out_ref[:, first : first + pair] = out.astype(jnp.bfloat16)


def attend(queries, keyvals, allowed):
    return pl.pallas_call(
        attend_kernel,
        out_shape=jax.ShapeDtypeStruct(queries.shape, jnp.bfloat16),
        name="attend_heads",
    )(queries, keyvals, allowed)


def student_hidden(widened_in, norm_gain, qkv_weight, out_weight, doc_ids):
    tok_rows, student_width = widened_in.shape[0] // 3, widened_in.shape[1]
    student_f = widened_in[tok_rows : 2 * tok_rows].astype(jnp.float32)
    normed = normed_rows(widened_in, norm_gain)
    widened = jnp.dot(
        normed, qkv_weight[:, student_width:], preferred_element_type=jnp.float32
    ).astype(jnp.bfloat16)
    queries = jnp.dot(
        normed[tok_rows : 2 * tok_rows],
        qkv_weight[:, :student_width],
        preferred_element_type=jnp.float32,
    ).astype(jnp.bfloat16)
    first_pos = lax.axis_index(COL) * tok_rows
    query_pos = first_pos + jnp.arange(tok_rows, dtype=jnp.int32)
    key_pos = first_pos - tok_rows + jnp.arange(3 * tok_rows, dtype=jnp.int32)
    filler = jnp.full((tok_rows,), -1, jnp.int32)
    padded_docs = jnp.concatenate([filler, doc_ids, filler])
    query_docs = lax.dynamic_slice_in_dim(doc_ids, first_pos, tok_rows)
    key_docs = lax.dynamic_slice_in_dim(padded_docs, first_pos, 3 * tok_rows)
    allowed = (query_docs[:, None] == key_docs[None, :]) & (
        jnp.abs(query_pos[:, None] - key_pos[None, :]) <= tok_rows
    )
    attended = attend(queries, widened, allowed.astype(jnp.float32))
    return (student_f + jnp.dot(attended, out_weight, preferred_element_type=jnp.float32)).astype(
        jnp.bfloat16
    )


def body(
    context_heads,
    teacher_proj,
    teacher_resid,
    student_in,
    norm_gain,
    qkv_weight,
    out_weight,
    head_weight,
    token_ids,
    doc_ids,
):
    tok_rows, student_width = student_in.shape
    row_tokens, depth = context_heads.shape
    out_width = teacher_resid.shape[1]
    half_width = teacher_proj.shape[1] // 2
    y, xl, zh, zl, xh, core = (lax.axis_index(axis).astype(jnp.int32) for axis in AXES)
    z, owner = zh * 2 + zl, zh * 2 + xh

    keep = lax.dynamic_slice_in_dim(teacher_proj, zl * half_width, half_width, axis=1)
    give = lax.dynamic_slice_in_dim(teacher_proj, (1 - zl) * half_width, half_width, axis=1)
    across = (keep, flip(give, "zl"), flip(keep, "xl"), flip(give, "xl", "zl"))
    own, other = [], []
    whole, *nears = pack(across)
    whole = flip(whole, "core")
    for near in nears:
        along_y = [near] + [shift(near, ("y",), -step) for step in (1, 3, 2)]
        along_y = [along_y[i] for i in (0, 1, 3, 2)]
        own.append(along_y)
        other.append([whole] + [flip(piece, "core") for piece in along_y[1:]])

    by_core = context_heads.reshape(row_tokens // (2 * tok_rows), 2, tok_rows, depth)
    here, there = (
        lax.dynamic_index_in_dim(by_core, i, 1, keepdims=False).reshape(row_tokens // 2, depth)
        for i in (core, 1 - core)
    )
    heads = (here, flip(there, "core"), flip(here, "zl"), flip(there, "zl", "core"))

    by_owner = teacher_resid.reshape(tok_rows, 2, 2, 2, 2, half_width).transpose(1, 4, 2, 0, 3, 5)
    resid_cols = exchange(
        by_owner.reshape(8, tok_rows, 2 * half_width), ("zh", "zl", "xh")
    )

    before, after = neighbours(student_in)
    widened_in = jnp.concatenate([before, student_in, after])
    hidden = student_hidden(widened_in, norm_gain, qkv_weight, out_weight, doc_ids)
    prediction = jnp.dot(hidden, head_weight, preferred_element_type=jnp.float32)
    kept = jnp.where((token_ids < SPECIAL)[:, None], hidden, jnp.zeros_like(hidden))
    kept = jnp.stack([kept, flip(kept, "xh")])
    from_z = [shift(kept, Z, far) for far in (1, 2, 3)]
    kept = jnp.stack([kept, *from_z])

    steps = jnp.arange(4, dtype=jnp.int32)
    pair = jnp.arange(2, dtype=jnp.int32)
    slots = (
        jnp.bitwise_xor((y + steps) % 4, owner)[:, None] * 2
        + jnp.bitwise_xor(jnp.bitwise_xor(xl, core), pair)[None]
    ).reshape(8)
    places = (
        ((z - steps) % 4)[:, None] * 2 + jnp.bitwise_xor(xh, pair)[None, :]
    ).reshape(8)
    places = jnp.concatenate([places, core.reshape(1)])
    weight = jnp.concatenate(
        [
            lax.dynamic_slice_in_dim(
                head_weight, (owner * 4 + half * 2 + zl) * half_width, half_width, axis=1
            )
            for half in (core, 1 - core)
        ],
        axis=1,
    )
    sent = []
    for chunk in range(CHUNKS):
        sent.append(teacher_partials(slots, heads, own[chunk], other[chunk], chunk))
    everyone = math.prod(SIZES)
    parts = []
    for chunk in range(CHUNKS):
        for far in range(4):
            axes = ("zh",) * (far // 2) + ("xh",) * (far % 2)
            part = sent[chunk][far]
            parts.append(flip(part, *axes) if axes else part)
    targets, product, give = gradient_term(places, kept, parts, weight, resid_cols)
    product = product + flip(give, "core")
    grad_pieces = exchange(product.reshape(everyone, student_width // everyone, half_width), AXES)
    head_grad = sum_rows([grad_pieces], out_width, 1.0 / row_tokens)
    targets = [targets[0]] + [shift(targets[far], Z, -far) for far in (1, 2, 3)]
    near, far_half = regroup(targets)
    pieces = (near, flip(far_half, "xh"))
    from_z = (z + steps) % 4
    columns = [
        (
            (from_z // 2 * 8 + (xh ^ half) * 4 + from_z % 2)[:, None]
            + jnp.bitwise_xor(core, pair)[None] * 2
        ).reshape(8)
        for half in range(2)
    ]
    target = place_columns(jnp.concatenate(columns) * half_width, pieces, out_width)
    return (target, prediction, head_grad)


def solution(mesh):
    fine = Mesh(mesh.devices.reshape(SIZES), AXES)
    row, col, whole = (("y", "xl"), COL, AXES)
    return jax.shard_map(
        body,
        mesh=fine,
        in_specs=(
            P(row, col),
            P(col, row),
            P(whole, None),
            P(whole, None),
            P(),
            P(),
            P(),
            P(),
            P(whole),
            P(row),
        ),
        out_specs=(P(whole, None), P(whole, None), P(whole, None)),
        check_vma=False,
    )
```

```python
import math

import jax
import jax.numpy as jnp
from jax import lax
from jax.experimental import pallas as pl
from jax.experimental.pallas import tpu as pltpu
from jax.sharding import Mesh
from jax.sharding import PartitionSpec as P

HEAD_DIM = 64
SPECIAL = 128000

AXES = ("y", "xl", "zh", "zl", "xh", "core")
SIZES = (4, 2, 2, 2, 2, 2)
COL = ("zh", "zl", "xh", "core")
Z = ("zh", "zl")
CHUNKS = 2


def exchange(blocks, axes):
    return lax.all_to_all(blocks, axes, 0, 0, tiled=True)


def shift(array, axes, step):
    size = math.prod(lax.axis_size(axis) for axis in axes)
    return lax.ppermute(array, axes, [(i, (i + step) % size) for i in range(size)])


def flip(array, *axes):
    last = 2 ** len(axes) - 1
    return lax.ppermute(array, axes, [(i, last - i) for i in range(last + 1)])


def partial_kernel(slot_ref, *refs):
    heads, weights, outs = refs[:4], refs[4:12], refs[12:16]
    sorted_ref, total_ref = refs[16:]
    width = outs[0].shape[1] // 2

    @pl.when(pl.program_id(0) == 0)
    def _():
        for step in range(4):
            for near in range(2):
                slot = slot_ref[step * 2 + near]
                lanes = pl.ds(pl.multiple_of((slot % 2) * width, width), width)
                for side in range(2):
                    for half in range(2):
                        sorted_ref[slot // 2, side, half, :, lanes] = weights[side * 4 + step][
                            near, half
                        ]

    def step(far, carry):
        total = None
        for side in range(2):
            for half in range(2):
                term = jnp.dot(
                    heads[half * 2 + side][...],
                    sorted_ref[far, side, half],
                    preferred_element_type=jnp.float32,
                ).astype(jnp.bfloat16)
                term = term.astype(jnp.float32)
                total = term if total is None else total + term
        total_ref[far] = total.astype(jnp.bfloat16)
        return carry

    lax.fori_loop(0, 4, step, 0)
    for far in range(4):
        outs[far][...] = total_ref[far]


def teacher_partials(slots, heads, own, other, chunk):
    tokens, depth = heads[0].shape
    width = own[0].shape[3]
    rows = 512
    weight_spec = pl.BlockSpec(own[0].shape, lambda i, _: (0, 0, 0, 0))
    return pl.pallas_call(
        partial_kernel,
        out_shape=[jax.ShapeDtypeStruct((tokens, 2 * width), jnp.bfloat16)] * 4,
        grid_spec=pltpu.PrefetchScalarGridSpec(
            num_scalar_prefetch=1,
            grid=(tokens // rows,),
            in_specs=[pl.BlockSpec((rows, depth), lambda i, _: (i, 0))] * 4
            + [weight_spec] * 4
            + [pl.BlockSpec((None, *own[0].shape), lambda i, _: (chunk, 0, 0, 0, 0))]
            + [
                pl.BlockSpec(x.shape, lambda i, _, n=x.ndim: (0,) * n)
                for x in other[1:]
            ],
            out_specs=[pl.BlockSpec((rows, 2 * width), lambda i, _: (i, 0))] * 4,
            scratch_shapes=[
                pltpu.VMEM((4, 2, 2, depth, 2 * width), jnp.bfloat16),
                pltpu.VMEM((4, rows, 2 * width), jnp.bfloat16),
            ],
        ),
        compiler_params=pltpu.CompilerParams(vmem_limit_bytes=58 * 1024 * 1024),
        name="teacher_partials",
    )(slots, *heads, *own, *other)


def pack_kernel(*refs):
    pieces, whole_ref, outs = refs[:4], refs[4], refs[5:]
    width = outs[0].shape[3]
    for chunk, out_ref in enumerate(outs):
        for i in range(4):
            piece = pieces[i][:, chunk * width : (chunk + 1) * width]
            out_ref[i // 2, i % 2] = piece
            whole_ref[chunk, i // 2, i % 2] = piece


def pack(pieces):
    depth, wide = pieces[0].shape
    shape = (2, 2, depth, wide // CHUNKS)
    return pl.pallas_call(
        pack_kernel,
        out_shape=[
            jax.ShapeDtypeStruct((CHUNKS, *shape), pieces[0].dtype),
            *[jax.ShapeDtypeStruct(shape, pieces[0].dtype)] * CHUNKS,
        ],
        name="pack",
    )(*pieces)


def regroup_kernel(*refs):
    for half, out_ref in enumerate(refs[4:]):
        for far in range(4):
            out_ref[far] = refs[far][half]


def regroup(pieces):
    shape = (4, *pieces[0].shape[1:])
    return pl.pallas_call(
        regroup_kernel,
        out_shape=[jax.ShapeDtypeStruct(shape, pieces[0].dtype)] * 2,
        name="regroup",
    )(*pieces)


def target_kernel(place_ref, *refs):
    parts, resid_ref, targets = refs[: 4 * CHUNKS], refs[4 * CHUNKS], refs[-4:]
    rows, wide = resid_ref.shape[1:]
    width = wide // 2
    piece = width // CHUNKS
    core = place_ref[8]
    for far in range(4):
        for half in range(2):
            block = place_ref[far * 2 + half]
            start = pl.multiple_of(block * rows, rows)
            for side in range(2):
                column = pl.multiple_of((core if side == 0 else 1 - core) * width, width)
                resid = resid_ref[block, :, pl.ds(column, width)].astype(jnp.float32)
                sums = []
                for chunk in range(CHUNKS):
                    total = None
                    for source in range(4):
                        lanes = slice(side * piece, (side + 1) * piece)
                        term = parts[chunk * 4 + source][pl.ds(start, rows), lanes]
                        term = term.astype(jnp.float32)
                        total = term if total is None else total + term
                    sums.append(total)
                target = (resid + jnp.concatenate(sums, axis=1)).astype(jnp.bfloat16)
                targets[far][half, :, side * width : (side + 1) * width] = target


def whole_spec(x):
    return pl.BlockSpec(x.shape, lambda i, _: (0,) * len(x.shape))


def make_targets(places, parts, resid):
    piece = jax.ShapeDtypeStruct((2, *resid.shape[1:]), jnp.bfloat16)
    return pl.pallas_call(
        target_kernel,
        out_shape=[piece] * 4,
        grid_spec=pltpu.PrefetchScalarGridSpec(
            num_scalar_prefetch=1,
            grid=(1,),
            in_specs=[whole_spec(x) for x in (*parts, resid)],
            out_specs=[whole_spec(piece)] * 4,
        ),
        compiler_params=pltpu.CompilerParams(vmem_limit_bytes=58 * 1024 * 1024),
        name="make_targets",
    )(places, *parts, resid)


def gradient_kernel(kept_ref, weight_ref, *refs):
    targets, (own_ref, give_ref), product_ref = refs[:4], refs[4:6], refs[6]
    rows, wide = targets[0].shape[1:]
    for far in range(4):
        tokens = kept_ref[far].reshape(2 * rows, -1)
        wanted = targets[far][...].reshape(2 * rows, wide).astype(jnp.float32)
        predicted = jnp.dot(tokens, weight_ref[...], preferred_element_type=jnp.float32)
        error = (predicted - wanted).astype(jnp.bfloat16)
        term = lax.dot_general(
            tokens, error, (((0,), (0,)), ((), ())), preferred_element_type=jnp.float32
        )
        if far == 0:
            product_ref[...] = term
        elif far < 3:
            product_ref[...] += term
        else:
            term = product_ref[...] + term
            own_ref[...] = term[:, : wide // 2]
            give_ref[...] = term[:, wide // 2 :]


def gradient_term(kept, weight, targets):
    half = jax.ShapeDtypeStruct((weight.shape[0], weight.shape[1] // 2), jnp.float32)
    return pl.pallas_call(
        gradient_kernel,
        out_shape=[half] * 2,
        scratch_shapes=[pltpu.VMEM(weight.shape, jnp.float32)],
        compiler_params=pltpu.CompilerParams(vmem_limit_bytes=58 * 1024 * 1024),
        name="gradient_term",
    )(kept, weight, *targets)


def regroup_kernel(*refs):
    for half, out_ref in enumerate(refs[4:]):
        for far in range(4):
            out_ref[far] = refs[far][half]


def regroup(pieces):
    shape = (4, *pieces[0].shape[1:])
    return pl.pallas_call(
        regroup_kernel,
        out_shape=[jax.ShapeDtypeStruct(shape, pieces[0].dtype)] * 2,
        name="regroup",
    )(*pieces)


def place_kernel(column_ref, *refs):
    out_ref = refs[-1]
    width = refs[0].shape[2] // 2
    for i, ref in enumerate(refs[:-1]):
        for far in range(4):
            for side in range(2):
                column = pl.multiple_of(column_ref[(i * 4 + far) * 2 + side], width)
                out_ref[:, pl.ds(column, width)] = ref[far, :, side * width : (side + 1) * width]


def place_columns(columns, pieces, out_width):
    rows = pieces[0].shape[1]
    return pl.pallas_call(
        place_kernel,
        out_shape=jax.ShapeDtypeStruct((rows, out_width), pieces[0].dtype),
        grid_spec=pltpu.PrefetchScalarGridSpec(
            num_scalar_prefetch=1,
            grid=(1,),
            in_specs=[pl.BlockSpec(x.shape, lambda i, _: (0, 0, 0)) for x in pieces],
            out_specs=pl.BlockSpec((rows, out_width), lambda i, _: (0, 0)),
        ),
        name="place_columns",
    )(columns, *pieces)


def sum_kernel(scale, *refs):
    out_ref = refs[-1]
    count, _, width = refs[0].shape
    groups = 16
    for chunk, ref in enumerate(refs[:-1]):
        for place in range(groups):
            zh, zl, owner = place // 8, place // 4 % 2, place % 4
            total = ref[place]
            for i in range(1, count // groups):
                total = total + ref[i * groups + place]
            column = ((zh * 8 + owner * 2 + zl) * (len(refs) - 1) + chunk) * width
            out_ref[:, column : column + width] = total * scale


def sum_rows(pieces, out_width, scale):
    rows = pieces[0].shape[1]
    return pl.pallas_call(
        lambda *refs: sum_kernel(scale, *refs),
        out_shape=jax.ShapeDtypeStruct((rows, out_width), jnp.float32),
        name="sum_rows",
    )(*pieces)


def neighbours(array):
    return shift(array, COL, 1), shift(array, COL, -1)


def normed_rows(rows, norm_gain):
    rows_f = rows.astype(jnp.float32)
    mean_sq = jnp.mean(rows_f * rows_f, axis=-1, keepdims=True)
    return (rows_f * lax.rsqrt(mean_sq + 1e-05) * norm_gain.astype(jnp.float32)).astype(
        jnp.bfloat16
    )


def attend_kernel(query_ref, keyval_ref, allowed_ref, out_ref):
    tok_rows, width = query_ref.shape
    pair = 2 * HEAD_DIM
    allowed = allowed_ref[...] > 0.0
    lane = lax.broadcasted_iota(jnp.int32, (tok_rows, pair), 1)
    for first in range(0, width, pair):
        queries = query_ref[:, first : first + pair]
        keys = keyval_ref[:, first : first + pair]
        values = keyval_ref[:, width + first : width + first + pair]
        mixed = []
        for head in range(2):
            inside = (lane < HEAD_DIM) if head == 0 else (lane >= HEAD_DIM)
            mine = jnp.where(inside, queries.astype(jnp.float32), 0.0).astype(jnp.bfloat16)
            scores = lax.dot_general(
                mine, keys, (((1,), (1,)), ((), ())), preferred_element_type=jnp.float32
            ) * (1.0 / math.sqrt(HEAD_DIM))
            scores = jnp.where(allowed, scores, -jnp.inf)
            exp_scores = jnp.exp(scores - jnp.max(scores, axis=-1, keepdims=True))
            weights = exp_scores / jnp.sum(exp_scores, axis=-1, keepdims=True)
            mixed.append(
                jnp.dot(
                    weights.astype(jnp.bfloat16), values, preferred_element_type=jnp.float32
                )
            )
        out = jnp.where(lane < HEAD_DIM, mixed[0], mixed[1])
        out_ref[:, first : first + pair] = out.astype(jnp.bfloat16)


def attend(queries, keyvals, allowed):
    return pl.pallas_call(
        attend_kernel,
        out_shape=jax.ShapeDtypeStruct(queries.shape, jnp.bfloat16),
        name="attend_heads",
    )(queries, keyvals, allowed)


def student_hidden(widened_in, norm_gain, qkv_weight, out_weight, doc_ids):
    tok_rows, student_width = widened_in.shape[0] // 3, widened_in.shape[1]
    student_f = widened_in[tok_rows : 2 * tok_rows].astype(jnp.float32)
    normed = normed_rows(widened_in, norm_gain)
    widened = jnp.dot(
        normed, qkv_weight[:, student_width:], preferred_element_type=jnp.float32
    ).astype(jnp.bfloat16)
    queries = jnp.dot(
        normed[tok_rows : 2 * tok_rows],
        qkv_weight[:, :student_width],
        preferred_element_type=jnp.float32,
    ).astype(jnp.bfloat16)
    first_pos = lax.axis_index(COL) * tok_rows
    query_pos = first_pos + jnp.arange(tok_rows, dtype=jnp.int32)
    key_pos = first_pos - tok_rows + jnp.arange(3 * tok_rows, dtype=jnp.int32)
    filler = jnp.full((tok_rows,), -1, jnp.int32)
    padded_docs = jnp.concatenate([filler, doc_ids, filler])
    query_docs = lax.dynamic_slice_in_dim(doc_ids, first_pos, tok_rows)
    key_docs = lax.dynamic_slice_in_dim(padded_docs, first_pos, 3 * tok_rows)
    allowed = (query_docs[:, None] == key_docs[None, :]) & (
        jnp.abs(query_pos[:, None] - key_pos[None, :]) <= tok_rows
    )
    attended = attend(queries, widened, allowed.astype(jnp.float32))
    return (student_f + jnp.dot(attended, out_weight, preferred_element_type=jnp.float32)).astype(
        jnp.bfloat16
    )


def body(
    context_heads,
    teacher_proj,
    teacher_resid,
    student_in,
    norm_gain,
    qkv_weight,
    out_weight,
    head_weight,
    token_ids,
    doc_ids,
):
    tok_rows, student_width = student_in.shape
    row_tokens, depth = context_heads.shape
    out_width = teacher_resid.shape[1]
    half_width = teacher_proj.shape[1] // 2
    y, xl, zh, zl, xh, core = (lax.axis_index(axis).astype(jnp.int32) for axis in AXES)
    z, owner = zh * 2 + zl, zh * 2 + xh

    keep = lax.dynamic_slice_in_dim(teacher_proj, zl * half_width, half_width, axis=1)
    give = lax.dynamic_slice_in_dim(teacher_proj, (1 - zl) * half_width, half_width, axis=1)
    across = (keep, flip(give, "zl"), flip(keep, "xl"), flip(give, "xl", "zl"))
    own, other = [], []
    whole, *nears = pack(across)
    whole = flip(whole, "core")
    for near in nears:
        along_y = [near] + [shift(near, ("y",), -step) for step in (1, 3, 2)]
        along_y = [along_y[i] for i in (0, 1, 3, 2)]
        own.append(along_y)
        other.append([whole] + [flip(piece, "core") for piece in along_y[1:]])

    by_core = context_heads.reshape(row_tokens // (2 * tok_rows), 2, tok_rows, depth)
    here, there = (
        lax.dynamic_index_in_dim(by_core, i, 1, keepdims=False).reshape(row_tokens // 2, depth)
        for i in (core, 1 - core)
    )
    heads = (here, flip(there, "core"), flip(here, "zl"), flip(there, "zl", "core"))

    by_owner = teacher_resid.reshape(tok_rows, 2, 2, 2, 2, half_width).transpose(1, 4, 2, 0, 3, 5)
    resid_cols = exchange(
        by_owner.reshape(8, tok_rows, 2 * half_width), ("zh", "zl", "xh")
    )

    before, after = neighbours(student_in)
    widened_in = jnp.concatenate([before, student_in, after])
    hidden = student_hidden(widened_in, norm_gain, qkv_weight, out_weight, doc_ids)
    prediction = jnp.dot(hidden, head_weight, preferred_element_type=jnp.float32)
    kept = jnp.where((token_ids < SPECIAL)[:, None], hidden, jnp.zeros_like(hidden))
    kept = jnp.stack([kept, flip(kept, "xh")])
    from_z = [shift(kept, Z, far) for far in (1, 2, 3)]
    kept = jnp.stack([kept, *from_z])

    steps = jnp.arange(4, dtype=jnp.int32)
    pair = jnp.arange(2, dtype=jnp.int32)
    slots = (
        jnp.bitwise_xor((y + steps) % 4, owner)[:, None] * 2
        + jnp.bitwise_xor(jnp.bitwise_xor(xl, core), pair)[None]
    ).reshape(8)
    places = (
        ((z - steps) % 4)[:, None] * 2 + jnp.bitwise_xor(xh, pair)[None, :]
    ).reshape(8)
    places = jnp.concatenate([places, core.reshape(1)])
    weight = jnp.concatenate(
        [
            lax.dynamic_slice_in_dim(
                head_weight, (owner * 4 + half * 2 + zl) * half_width, half_width, axis=1
            )
            for half in (core, 1 - core)
        ],
        axis=1,
    )
    sent = []
    for chunk in range(CHUNKS):
        sent.append(teacher_partials(slots, heads, own[chunk], other[chunk], chunk))
    everyone = math.prod(SIZES)
    parts = []
    for chunk in range(CHUNKS):
        for far in range(4):
            axes = ("zh",) * (far // 2) + ("xh",) * (far % 2)
            part = sent[chunk][far]
            parts.append(flip(part, *axes) if axes else part)
    targets = make_targets(places, parts, resid_cols)
    product, give = gradient_term(kept, weight, targets)
    product = product + flip(give, "core")
    grad_pieces = exchange(product.reshape(everyone, student_width // everyone, half_width), AXES)
    head_grad = sum_rows([grad_pieces], out_width, 1.0 / row_tokens)
    targets = [targets[0]] + [shift(targets[far], Z, -far) for far in (1, 2, 3)]
    near, far_half = regroup(targets)
    pieces = (near, flip(far_half, "xh"))
    from_z = (z + steps) % 4
    columns = [
        (
            (from_z // 2 * 8 + (xh ^ half) * 4 + from_z % 2)[:, None]
            + jnp.bitwise_xor(core, pair)[None] * 2
        ).reshape(8)
        for half in range(2)
    ]
    target = place_columns(jnp.concatenate(columns) * half_width, pieces, out_width)
    return (target, prediction, head_grad)


def solution(mesh):
    fine = Mesh(mesh.devices.reshape(SIZES), AXES)
    row, col, whole = (("y", "xl"), COL, AXES)
    return jax.shard_map(
        body,
        mesh=fine,
        in_specs=(
            P(row, col),
            P(col, row),
            P(whole, None),
            P(whole, None),
            P(),
            P(),
            P(),
            P(),
            P(whole),
            P(row),
        ),
        out_specs=(P(whole, None), P(whole, None), P(whole, None)),
        check_vma=False,
    )
```
